32 devices in a mesh: seq: 4 (over z), dp: 8 (over y, x, core).
Axes of the slice: x: 2, y: 2, z: 4, core: 2. Of those that a mesh axis runs over, the one named last changes fastest.
Arguments:
- hidden_in: bfloat16 [16, 2048, 1024], P('dp', 'seq'), may hold values from -6 to 6
- mixer_weights: float32 [1, 5, 1024, 1024], P(None, None, 'dp'), may hold values from -0.1875 to 0.1875
- channel_in_weights: float32 [1, 2, 1024, 2816], P(None, None, 'dp'), may hold values from -0.1875 to 0.1875
- channel_out_weights: float32 [1, 2816, 1024], P(None, 'dp'), may hold values from -0.109375 to 0.109375
- decay_rates: float32 [1, 8], replicated, may hold values from 0 to 0.034, as said below
- doc_lengths: int32 [16, 4], P('dp'), may hold values from 1 to 1024, 2048 in all within a row
- out_cotangent: bfloat16 [16, 2048, 1024], P('dp', 'seq'), may hold values from -6 to 6
Outputs:
- block_output: bfloat16 [16, 2048, 1024], P('dp', 'seq')
- input_gradient: float32 [16, 2048, 1024], P('dp', 'seq')
- mixer_gradient: float32 [1, 5, 1024, 1024], P(None, None, 'dp')
- channel_in_gradient: float32 [1, 2, 1024, 2816], P(None, None, 'dp')
- channel_out_gradient: float32 [1, 2816, 1024], P(None, 'dp')
The draws below stay inside these ranges and needn't reach their ends.
Inputs may be any that keep to these rules, and one draw needn't show every extreme that they name: `decay_rates`: positive decay rates. `doc_lengths`: each row's 4 lengths add up to 2048.
All inputs are finite; a program needn't handle non-finite values.
Results may differ from the reference program's by a relative error of at most 0.02.
Values may be sent and summed in bfloat16 or wider, within the bound.
No kernel may reach another device: no remote copies, remote signals or barrier semaphores. Data moves between devices by JAX's collectives and lax.ppermute only.
A program may use at most 256 MiB of HBM per device.

```python
import math
import jax
import jax.numpy as jnp
import numpy as np
from jax import lax

D = 1024
HEADS = 8
HEAD_DIM = 128
FF = 2816
LAYERS = 1
DOCS = 4
SEQLEN = 2048
TOK_SEQ = 512
ROWS = 16


def draw_decay_rates(key, part):
    pick_key = jax.random.fold_in(key, 11)
    fast_key = jax.random.fold_in(key, 12)
    slow_key = jax.random.fold_in(key, 13)
    share = 0.5
    chooser = jax.random.uniform(pick_key, (LAYERS, HEADS), jnp.float32)
    fast = jnp.exp(jax.random.uniform(fast_key, (LAYERS, HEADS), jnp.float32, math.log(1.0 / 50.0), math.log(1.0 / 30.0)))
    slow = jnp.exp(jax.random.uniform(slow_key, (LAYERS, HEADS), jnp.float32, math.log(0.1 / SEQLEN), math.log(2.0 / SEQLEN)))
    return jnp.where(chooser < share, fast, slow).astype(jnp.float32)


def shard_levels(own_key, extent, pieces, smallest, high):
    level, own = 1.0, jax.random.fold_in(own_key, 6)
    for axis_at, shards_of in pieces:
        heights = jnp.exp(jax.random.uniform(jax.random.fold_in(own, axis_at), (shards_of,), jnp.float32, smallest / len(pieces), high / len(pieces)))
        level = level * jnp.repeat(heights, extent[axis_at] // shards_of).reshape([-1 if axis == axis_at else 1 for axis in range(len(extent))])
    return level


def length_profile(amount, total, reach, lean):
    loads = [(1 << 20) // math.isqrt(standing ** lean) + 1 for standing in range(2, amount + 1)]
    surplus, counts = total - reach - (amount - 1), [1] * (amount - 1)
    while surplus > 0:
        candidates = [i for i in range(amount - 1) if counts[i] < reach]
        whole, remaining = sum([loads[i] for i in candidates]), surplus
        for i in candidates:
            more = min(reach - counts[i], max(1, remaining * loads[i] // whole), surplus)
            counts[i] = counts[i] + more
            surplus = surplus - more
    return np.array([reach] + counts)


def ragged_sizes(own_key, amount, total, bound, skew):
    if amount == 2:
        one = jax.random.randint(own_key, (), max(1, total - bound), min(bound, total - 1) + 1)
        return jnp.stack([one, total - one])
    sizes = jnp.asarray(length_profile(amount, total, bound, skew), jnp.int32)
    twos = (amount - 1) // 2
    giver, receiver = sizes[1:1 + 2 * twos:2], sizes[2:2 + 2 * twos:2]
    margin = jnp.minimum(giver - 1, bound - receiver)
    passed = jax.random.randint(jax.random.fold_in(own_key, 1), (twos,), 0, 1 << 20) % (margin + 1)
    sizes = sizes.at[1:1 + 2 * twos:2].set(giver - passed).at[2:2 + 2 * twos:2].set(receiver + passed)
    return sizes[jax.random.permutation(jax.random.fold_in(own_key, 2), amount)]


def bell_draw(stream_key, dims, width, most, split=(), kind=jnp.bfloat16):
    loudness = shard_levels(stream_key, dims, split, -0.22, 0.18) if split else 1.0
    entries = jax.random.normal(stream_key, dims, jnp.float32) * width * loudness
    return jnp.minimum(jnp.maximum(entries, -most), most).astype(kind)


def setup_inputs(seed: int = 0) -> dict:
    splits = jax.random.split(jax.random.key(seed), 8)
    hidden_in = bell_draw(splits[0], (ROWS, SEQLEN, D), 1.0, 6.0, ((0, 8), (1, 4)))
    mixer_weights = bell_draw(splits[1], (LAYERS, 5, D, D), D ** -0.5, 0.1875, ((2, 8),), jnp.float32)
    channel_in_weights = bell_draw(splits[2], (LAYERS, 2, D, FF), D ** -0.5, 0.1875, ((2, 8),), jnp.float32)
    channel_out_weights = bell_draw(splits[3], (LAYERS, FF, D), FF ** -0.5, 0.109375, ((1, 8),), jnp.float32)
    decay_rates = draw_decay_rates(jax.random.fold_in(splits[7], 71), 0)
    doc_lengths = jax.vmap(lambda own: ragged_sizes(own, DOCS, SEQLEN, SEQLEN // 2, 2))(jax.random.split(splits[5], ROWS)).reshape((ROWS, DOCS)).astype(jnp.int32)
    out_cotangent = bell_draw(splits[6], (ROWS, SEQLEN, D), 1.0, 6.0, ((0, 8), (1, 4)))
    return dict(hidden_in=hidden_in, mixer_weights=mixer_weights, channel_in_weights=channel_in_weights, channel_out_weights=channel_out_weights, decay_rates=decay_rates, doc_lengths=doc_lengths, out_cotangent=out_cotangent)


EPS = 1e-06
FULL_PRECISION = lax.Precision.HIGHEST

@jax.custom_vjp
def low(v):
    return lax.optimization_barrier(v.astype(jnp.bfloat16)).astype(jnp.float32)

@jax.custom_vjp
def low_back(v):
    return v

def low_keep(v):
    return (low(v), None)

def low_pass(kept, grad):
    return (grad,)

def back_keep(v):
    return (v, None)

def back_low(kept, grad):
    return (low(grad),)
low.defvjp(low_keep, low_pass)
low_back.defvjp(back_keep, back_low)

def norm_rows(value_rows):
    return value_rows * lax.rsqrt(lax.optimization_barrier(jnp.mean(value_rows * value_rows, axis=-1, keepdims=True)) + EPS)

def swish(value_rows):
    return value_rows * jax.nn.sigmoid(value_rows)

def doc_index(doc_ends, places):
    compare = places.astype(jnp.int32)[None, :, None] >= doc_ends.astype(jnp.int32)[:, None, :]
    return lax.optimization_barrier(jnp.sum(compare.astype(jnp.int32), axis=-1, dtype=jnp.int32)).astype(jnp.int32)

def decay_tables(rates, doc_ends, start, count):
    float_kind = rates.dtype
    offsets = jnp.arange(count, dtype=jnp.int32)
    start = jnp.asarray(start, dtype=jnp.int32)
    doc_here = doc_index(doc_ends, start + offsets)
    before_place = jnp.full((1,), -1, dtype=jnp.int32) + start
    doc_before = doc_index(doc_ends, before_place)[:, 0]
    doc_last = doc_here[:, count - 1]
    distance = jnp.maximum(offsets[:, None] - offsets[None, :], 0).astype(float_kind)
    causal = offsets[:, None] >= offsets[None, :]
    linked = causal[None] & (doc_here[:, :, None] == doc_here[:, None, :])
    intra_vals = jnp.exp(-rates[None, :, None, None] * distance[None, None])
    intra = jnp.where(linked[:, None], intra_vals, jnp.zeros_like(intra_vals))
    ahead = (offsets + 1).astype(float_kind)
    behind = (count - 1 - offsets).astype(float_kind)
    entry_vals = jnp.exp(-rates[None, None, :] * ahead[None, :, None])
    entry = jnp.where((doc_here == doc_before[:, None])[:, :, None], entry_vals, jnp.zeros_like(entry_vals))
    leaving_vals = jnp.exp(-rates[None, None, :] * behind[None, :, None])
    leaving = jnp.where((doc_here == doc_last[:, None])[:, :, None], leaving_vals, jnp.zeros_like(leaving_vals))
    length_value = jnp.asarray(count, dtype=float_kind)
    passing_vals = jnp.exp(-rates * length_value)[None, :] + jnp.zeros((doc_last.shape[0], 1), float_kind)
    passing = jnp.where((doc_last == doc_before)[:, None], passing_vals, jnp.zeros_like(passing_vals))
    return (intra, entry, leaving, passing)

def block_out(per_head_queries, per_head_keys, per_head_values, tables, state_in):
    scores = jnp.einsum('rthd,rshd->rhts', per_head_queries, per_head_keys, precision=FULL_PRECISION) * tables[0]
    local_part = jnp.einsum('rhts,rshe->rthe', scores, per_head_values, precision=FULL_PRECISION)
    carried = jnp.einsum('rthd,rhde->rthe', per_head_queries, state_in, precision=FULL_PRECISION) * tables[1][..., None]
    return local_part + carried

def block_state(per_head_keys, per_head_values, tables):
    return jnp.einsum('rshd,rshe->rhde', per_head_keys * tables[2][..., None], per_head_values, precision=FULL_PRECISION)

def sequence_attention(per_head_queries, per_head_keys, per_head_values, rates, doc_ends):
    groups = per_head_queries.shape[0]
    blocks = SEQLEN // TOK_SEQ
    block_width = int(TOK_SEQ)

    def block_regrouping(value_rows):
        return value_rows.reshape(groups, blocks, block_width, HEADS, HEAD_DIM).transpose(1, 0, 2, 3, 4)

    def step_forward(state, items):
        query_block, key_block, value_block, block_index = items
        block_start = block_index.astype(jnp.int32) * jnp.asarray(block_width, dtype=jnp.int32)
        tables = decay_tables(rates, doc_ends, block_start, block_width)
        output = block_out(query_block, key_block, value_block, tables, state)
        state_next = tables[3][:, :, None, None] * state + block_state(key_block, value_block, tables)
        return (state_next.astype(state.dtype), output.astype(state.dtype))
    starting_state = jnp.zeros((groups, HEADS, HEAD_DIM, HEAD_DIM), per_head_queries.dtype)
    index_list = jnp.arange(blocks, dtype=jnp.int32)
    closing_state, output_rows = lax.scan(jax.checkpoint(step_forward), starting_state, (block_regrouping(per_head_queries), block_regrouping(per_head_keys), block_regrouping(per_head_values), index_list))
    return output_rows.transpose(1, 0, 2, 3, 4).reshape(groups * SEQLEN, D)

def project(left, right):
    return jnp.dot(left, right, preferred_element_type=jnp.float32, precision=FULL_PRECISION)

def forward(resid, mixer_weights, channel_in_weights, channel_out_weights, decay_rates, doc_ends):
    groups = resid.shape[0]
    mixer_low = low(mixer_weights)
    channel_low = low(channel_in_weights)
    down_low = low(channel_out_weights)
    flat = resid.reshape(groups * SEQLEN, D)
    head_shape = (groups, SEQLEN, HEADS, HEAD_DIM)
    for layer_index in range(LAYERS):
        normed = low(norm_rows(flat))
        query_pre = low_back(project(normed, mixer_low[layer_index, 0]))
        key_pre = low_back(project(normed, mixer_low[layer_index, 1]))
        value_pre = low_back(project(normed, mixer_low[layer_index, 2]))
        gate_pre = low_back(project(normed, mixer_low[layer_index, 3]))
        mixed = sequence_attention(swish(query_pre).reshape(head_shape), swish(key_pre).reshape(head_shape), value_pre.reshape(head_shape), decay_rates[layer_index], doc_ends)
        gated = low(low_back(norm_rows(mixed) * gate_pre))
        after_mixer = flat + low_back(project(gated, mixer_low[layer_index, 4]))
        normed_two = low(norm_rows(after_mixer))
        first = low_back(project(normed_two, channel_low[layer_index, 0]))
        second = low_back(project(normed_two, channel_low[layer_index, 1]))
        glu = low(low_back(first * second))
        flat = after_mixer + low_back(project(glu, down_low[layer_index]))
    return flat.reshape(groups, SEQLEN, D)

def reference(hidden_in, mixer_weights, channel_in_weights, channel_out_weights, decay_rates, doc_lengths, out_cotangent):
    group = math.gcd(int(ROWS), max(1, 4096 // int(SEQLEN)))
    steps = int(ROWS) // group
    mixer_wide = mixer_weights.astype(jnp.float32)
    channel_wide = channel_in_weights.astype(jnp.float32)
    down_wide = channel_out_weights.astype(jnp.float32)
    rates_wide = decay_rates.astype(jnp.float32)
    doc_ends = jnp.cumsum(doc_lengths.astype(jnp.int32), axis=1, dtype=jnp.int32).astype(jnp.int32).reshape(steps, group, DOCS)
    inputs = hidden_in.astype(jnp.float32).reshape(steps, group, SEQLEN, D)
    cotangents = out_cotangent.astype(jnp.float32).reshape(steps, group, SEQLEN, D)

    def one_group(totals, items):
        group_in, group_cot, group_ends = items

        def apply(value_rows, mixer, channel_in, channel_out):
            return forward(value_rows, mixer, channel_in, channel_out, rates_wide, group_ends)
        result, pullback = jax.vjp(apply, group_in, mixer_wide, channel_wide, down_wide)
        input_grad, mixer_grad, in_grad, out_grad = pullback(group_cot)
        totals = (totals[0] + mixer_grad.astype(totals[0].dtype), totals[1] + in_grad.astype(totals[1].dtype), totals[2] + out_grad.astype(totals[2].dtype))
        return (totals, (result.astype(jnp.bfloat16), input_grad.astype(jnp.float32)))
    zeros = (jnp.zeros(mixer_wide.shape, jnp.float32), jnp.zeros(channel_wide.shape, jnp.float32), jnp.zeros(down_wide.shape, jnp.float32))
    totals, (output_rows, input_grads) = lax.scan(one_group, zeros, (inputs, cotangents, doc_ends))
    return (output_rows.reshape(ROWS, SEQLEN, D), input_grads.reshape(ROWS, SEQLEN, D), totals[0], totals[1], totals[2])
```

```python
import functools

import jax
import jax.numpy as jnp
from jax import lax
from jax.experimental import pallas as pl
from jax.experimental.pallas import tpu as pltpu
from jax.sharding import PartitionSpec as P

EPS = 1e-06
LONGEST_DOC = 1024
LOW = jnp.bfloat16
WIDE = jnp.float32
VMEM_BYTES = 60 * 1024 * 1024


def dot(left, right, left_dim, right_dim):
    return lax.dot_general(
        left, right, (((left_dim,), (right_dim,)), ((), ())), preferred_element_type=WIDE
    )


def swish(value_rows):
    return value_rows * jax.nn.sigmoid(value_rows)


def swish_slope(value_rows):
    gate = jax.nn.sigmoid(value_rows)
    return gate * (1.0 + value_rows * (1.0 - gate))


def doc_bounds(lengths_ref, row, docs, start, count):
    last = start + count - 1
    end = jnp.int32(0)
    last_from = jnp.int32(0)
    entry_to = jnp.int32(0)
    found = jnp.int32(0)
    for index in range(docs):
        end = end + lengths_ref[row, index]
        last_from = jnp.where(end <= last, end, last_from)
        ends_later = end > start - 1
        entry_to = jnp.where(ends_later & (found == 0), end, entry_to)
        found = jnp.where(ends_later, 1, found)
    return last_from - start, entry_to - start


def doc_starts(lengths_ref, row, docs, start, places):
    end = jnp.int32(0)
    begin = jnp.full(places.shape, -start, jnp.int32)
    for index in range(docs):
        end = end + lengths_ref[row, index]
        begin = jnp.where(places >= end - start, end - start, begin)
    return begin


def state_kernel(docs, start_ref, rates_ref, lengths_ref, keys_ref, values_ref, state_ref):
    count, head_dim = keys_ref.shape[1], state_ref.shape[-1]
    last_from, _ = doc_bounds(lengths_ref, pl.program_id(0), docs, start_ref[0], count)
    places = lax.broadcasted_iota(jnp.int32, (count, 1), 0)
    for head in range(state_ref.shape[1]):
        span = slice(head * head_dim, (head + 1) * head_dim)
        leaving = jnp.where(
            places >= last_from,
            jnp.exp(-rates_ref[head] * (count - 1 - places).astype(WIDE)),
            0.0,
        )
        keys = (swish(keys_ref[0, :, span].astype(WIDE)) * leaving).astype(LOW)
        state_ref[0, head] = dot(keys, values_ref[0, :, span], 0, 0).astype(LOW)


def mixing_kernel(
    docs, tile, start_ref, rates_ref, lengths_ref, q_ref, k_ref, v_ref, out_ref, mask_ref
):
    count, features = q_ref.shape[1], q_ref.shape[2]
    heads = rates_ref.shape[0]
    head_dim = features // heads
    places = lax.broadcasted_iota(jnp.int32, (count, 1), 0)
    begin = doc_starts(lengths_ref, pl.program_id(0), docs, start_ref[0], places)
    across = lax.broadcasted_iota(jnp.int32, (count, count), 1)
    mask_ref[...] = ((across <= places) & (across >= begin)).astype(WIDE)
    centred = (places - count // 2).astype(WIDE)
    for head in range(heads):
        span = slice(head * head_dim, (head + 1) * head_dim)
        rate = rates_ref[head]
        queries = (swish(q_ref[0, :, span].astype(WIDE)) * jnp.exp(-rate * centred)).astype(LOW)
        keys = (swish(k_ref[0, :, span].astype(WIDE)) * jnp.exp(rate * centred)).astype(LOW)
        values = v_ref[0, :, span]
        for first in range(0, count, tile):
            upto = first + tile
            scores = dot(queries[first:upto], keys[:upto], 1, 1) * mask_ref[first:upto, :upto]
            out_ref[0, first:upto, span] = dot(scores.astype(LOW), values[:upto], 1, 0).astype(
                out_ref.dtype
            )


def finish_kernel(
    docs,
    start_ref,
    rates_ref,
    lengths_ref,
    q_ref,
    u_ref,
    part_ref,
    state_ref,
    mixed_ref,
    gated_ref,
    whole_ref,
):
    count, features = q_ref.shape[1], q_ref.shape[2]
    heads = rates_ref.shape[0]
    head_dim = features // heads
    _, entry_to = doc_bounds(lengths_ref, pl.program_id(0), docs, start_ref[0], count)
    places = lax.broadcasted_iota(jnp.int32, (count, 1), 0)
    for head in range(heads):
        span = slice(head * head_dim, (head + 1) * head_dim)
        entry = jnp.where(
            places < entry_to, jnp.exp(-rates_ref[head] * (places + 1).astype(WIDE)), 0.0
        )
        queries = (swish(q_ref[0, :, span].astype(WIDE)) * entry).astype(LOW)
        whole_ref[:, span] = part_ref[0, :, span].astype(WIDE) + dot(
            queries, state_ref[0, head], 1, 0
        )
    mixed = whole_ref[...]
    factor = lax.rsqrt(jnp.mean(mixed * mixed, axis=-1, keepdims=True) + EPS)
    mixed_ref[0] = mixed.astype(LOW)
    gated_ref[0] = (mixed * factor * u_ref[0].astype(WIDE)).astype(LOW)


def back_gate_kernel(
    docs,
    start_ref,
    rates_ref,
    lengths_ref,
    q_ref,
    u_ref,
    mixed_ref,
    dgated_ref,
    dmixed_ref,
    du_ref,
    grad_ref,
):
    count, features = q_ref.shape[1], q_ref.shape[2]
    heads = rates_ref.shape[0]
    head_dim = features // heads
    mixed = mixed_ref[0].astype(WIDE)
    factor = lax.rsqrt(jnp.mean(mixed * mixed, axis=-1, keepdims=True) + EPS)
    dgated = dgated_ref[0].astype(WIDE)
    du_ref[0] = (dgated * mixed * factor).astype(LOW)
    upstream = dgated * u_ref[0].astype(WIDE)
    inner = jnp.sum(upstream * mixed, axis=-1, keepdims=True)
    dmixed_ref[0] = (
        factor * upstream - (factor * factor * factor / features * inner) * mixed
    ).astype(LOW)
    _, entry_to = doc_bounds(lengths_ref, pl.program_id(0), docs, start_ref[0], count)
    places = lax.broadcasted_iota(jnp.int32, (count, 1), 0)
    for head in range(heads):
        span = slice(head * head_dim, (head + 1) * head_dim)
        entry = jnp.where(
            places < entry_to, jnp.exp(-rates_ref[head] * (places + 1).astype(WIDE)), 0.0
        )
        queries = (swish(q_ref[0, :, span].astype(WIDE)) * entry).astype(LOW)
        grad_ref[0, head] = dot(queries, dmixed_ref[0, :, span], 0, 0).astype(LOW)


def back_mixing_kernel(
    docs,
    tile,
    start_ref,
    rates_ref,
    lengths_ref,
    q_ref,
    k_ref,
    v_ref,
    dmixed_ref,
    state_ref,
    dq_ref,
    dk_ref,
    dv_ref,
    mask_ref,
    turned_ref,
):
    count, features = q_ref.shape[1], q_ref.shape[2]
    heads = rates_ref.shape[0]
    head_dim = features // heads
    row = pl.program_id(0)
    start = start_ref[0]
    _, entry_to = doc_bounds(lengths_ref, row, docs, start, count)
    places = lax.broadcasted_iota(jnp.int32, (count, 1), 0)
    begin = doc_starts(lengths_ref, row, docs, start, places)
    across = lax.broadcasted_iota(jnp.int32, (count, count), 1)
    mask_ref[...] = ((across <= places) & (across >= begin)).astype(WIDE)
    flat = lax.broadcasted_iota(jnp.int32, (1, count), 1)
    begin = doc_starts(lengths_ref, row, docs, start, flat)
    down = lax.broadcasted_iota(jnp.int32, (count, count), 0)
    turned_ref[...] = ((down <= flat) & (down >= begin)).astype(WIDE)
    centred = (places - count // 2).astype(WIDE)
    for head in range(heads):
        span = slice(head * head_dim, (head + 1) * head_dim)
        rate = rates_ref[head]
        query_decay, key_decay = jnp.exp(-rate * centred), jnp.exp(rate * centred)
        entry = jnp.where(places < entry_to, jnp.exp(-rate * (places + 1).astype(WIDE)), 0.0)
        query_pre = q_ref[0, :, span].astype(WIDE)
        queries = (swish(query_pre) * query_decay).astype(LOW)
        keys = (swish(k_ref[0, :, span].astype(WIDE)) * key_decay).astype(LOW)
        values = v_ref[0, :, span]
        upstream = dmixed_ref[0, :, span]
        slope = swish_slope(query_pre)
        for first in range(0, count, tile):
            upto = first + tile
            grads = dot(upstream[first:upto], values[:upto], 1, 1) * mask_ref[first:upto, :upto]
            dq = dot(grads.astype(LOW), keys[:upto], 1, 0) * query_decay[first:upto]
            carried = dot(upstream[first:upto], state_ref[0, head], 1, 1) * entry[first:upto]
            dq_ref[0, first:upto, span] = ((dq + carried) * slope[first:upto]).astype(LOW)
            turned = turned_ref[first:upto, first:]
            grads = dot(values[first:upto], upstream[first:], 1, 1) * turned
            dk = dot(grads.astype(LOW), queries[first:], 1, 0) * key_decay[first:upto]
            dk_ref[0, first:upto, span] = dk.astype(LOW)
            scores = dot(keys[first:upto], queries[first:], 1, 1) * turned
            dv_ref[0, first:upto, span] = dot(scores.astype(LOW), upstream[first:], 1, 0).astype(LOW)


def back_finish_kernel(
    docs,
    start_ref,
    rates_ref,
    lengths_ref,
    k_ref,
    v_ref,
    dk_part_ref,
    dv_part_ref,
    grad_ref,
    dk_ref,
    dv_ref,
):
    count, features = k_ref.shape[1], k_ref.shape[2]
    heads = rates_ref.shape[0]
    head_dim = features // heads
    last_from, _ = doc_bounds(lengths_ref, pl.program_id(0), docs, start_ref[0], count)
    places = lax.broadcasted_iota(jnp.int32, (count, 1), 0)
    for head in range(heads):
        span = slice(head * head_dim, (head + 1) * head_dim)
        leaving = jnp.where(
            places >= last_from,
            jnp.exp(-rates_ref[head] * (count - 1 - places).astype(WIDE)),
            0.0,
        )
        key_pre = k_ref[0, :, span].astype(WIDE)
        grad = grad_ref[0, head]
        dk = dot(v_ref[0, :, span], grad, 1, 1) * leaving + dk_part_ref[0, :, span].astype(WIDE)
        dk_ref[0, :, span] = (dk * swish_slope(key_pre)).astype(LOW)
        keys = (swish(key_pre) * leaving).astype(LOW)
        dv = dot(keys, grad, 1, 0) + dv_part_ref[0, :, span].astype(WIDE)
        dv_ref[0, :, span] = dv.astype(LOW)


def row_call(kernel, scalars, inputs, outputs, scratch, flops):
    rows = inputs[0].shape[0]

    def spec(array):
        rest = len(array.shape) - 1
        return pl.BlockSpec((1, *array.shape[1:]), lambda i, *_: (i,) + (0,) * rest)

    size = sum(a.size * a.dtype.itemsize for a in inputs)
    size += sum(o.size * o.dtype.itemsize for o in outputs)
    return pl.pallas_call(
        kernel,
        out_shape=outputs,
        grid_spec=pltpu.PrefetchScalarGridSpec(
            num_scalar_prefetch=len(scalars),
            grid=(rows,),
            in_specs=[spec(a) for a in inputs],
            out_specs=[spec(o) for o in outputs],
            scratch_shapes=scratch,
        ),
        compiler_params=pltpu.CompilerParams(vmem_limit_bytes=VMEM_BYTES),
        cost_estimate=pl.CostEstimate(flops=flops, bytes_accessed=size, transcendentals=0),
    )(*scalars, *inputs)


def passed_along(value, steps):
    count = lax.axis_size("seq")
    leading, last = max(0, -steps), min(count, count - steps)
    return lax.ppermute(value, "seq", [(source, source + steps) for source in range(leading, last)])


def carried(local_state, passing, tokens, steps):
    hops = min((LONGEST_DOC - 2) // tokens + 1, lax.axis_size("seq") - 1)
    message, total = local_state, jnp.zeros(local_state.shape, WIDE)
    for hop in range(hops):
        received = passed_along(message, steps)
        total = total + received.astype(WIDE)
        message = (passing[..., None, None] * received.astype(WIDE)).astype(LOW)
    return total.astype(LOW)


def place_kernel(order_ref, *refs):
    count = len(refs) - 4
    pieces, out_ref, whole_ref, in_sem, out_sem = refs[:count], *refs[count:]
    rows = pieces[0].shape[1]

    def into(index):
        at = pl.ds(pl.multiple_of(order_ref[index] * rows, rows), rows)
        return pltpu.make_async_copy(pieces[index], whole_ref.at[:, at, :], in_sem.at[index])

    def out(index):
        at = pl.ds(pl.multiple_of(order_ref[index] * rows, rows), rows)
        return pltpu.make_async_copy(
            whole_ref.at[:, at, :], out_ref.at[:, at, :], out_sem.at[index]
        )

    for index in range(count):
        into(index).start()
    for index in range(count):
        into(index).wait()
        out(index).start()
    for index in range(count):
        out(index).wait()


def placed(pieces, order):
    count, (layers, rows, columns) = len(pieces), pieces[0].shape
    shape = (layers, count * rows, columns)
    size = count * pieces[0].size * pieces[0].dtype.itemsize
    return pl.pallas_call(
        place_kernel,
        out_shape=jax.ShapeDtypeStruct(shape, pieces[0].dtype),
        grid_spec=pltpu.PrefetchScalarGridSpec(
            num_scalar_prefetch=1,
            grid=(),
            in_specs=[pl.BlockSpec(memory_space=pl.ANY)] * count,
            out_specs=pl.BlockSpec(memory_space=pl.ANY),
            scratch_shapes=[
                pltpu.VMEM(shape, pieces[0].dtype),
                pltpu.SemaphoreType.DMA((count,)),
                pltpu.SemaphoreType.DMA((count,)),
            ],
        ),
        compiler_params=pltpu.CompilerParams(vmem_limit_bytes=VMEM_BYTES),
        cost_estimate=pl.CostEstimate(flops=0, bytes_accessed=2 * size, transcendentals=0),
    )(order, *pieces)


def side_steps(device):
    return (2, 4) if device % 2 == 0 else (4, 2)


def moved(value, kind):
    count = lax.axis_size("dp")
    if kind == "core":
        pairs = [(device, device ^ 1) for device in range(count)]
    else:
        pairs = [(device, device ^ side_steps(device)[kind]) for device in range(count)]
    return lax.ppermute(value, "dp", pairs)


def block_order():
    device = lax.axis_index("dp")
    table = []
    for index in range(8):
        row = []
        for mine in (index, index ^ 1):
            first, second = side_steps(mine)
            row += [mine, mine ^ first, mine ^ second, mine ^ first ^ second]
        table.append(row)
    return jnp.asarray(table, jnp.int32)[device]


def gathered(piece):
    if lax.axis_size("dp") != 8:
        return lax.all_gather(piece, "dp", axis=1, tiled=True)
    first = moved(piece, 0)
    second = moved(piece, 1)
    across = moved(first, 1)
    mine = [piece, first, second, across]
    other = [moved(part, "core") for part in mine]
    return placed(mine + other, block_order())


def order_kernel(order_ref, in_ref, out_ref):
    out_ref[...] = in_ref[...]


def ordered(value, order):
    count, (tokens, features) = order.shape[0], value.shape
    width = features // count
    return pl.pallas_call(
        order_kernel,
        out_shape=jax.ShapeDtypeStruct(value.shape, value.dtype),
        grid_spec=pltpu.PrefetchScalarGridSpec(
            num_scalar_prefetch=1,
            grid=(count,),
            in_specs=[pl.BlockSpec((tokens, width), lambda i, order: (0, order[i]))],
            out_specs=pl.BlockSpec((tokens, width), lambda i, order: (0, i)),
        ),
        cost_estimate=pl.CostEstimate(
            flops=0, bytes_accessed=2 * value.size * 2, transcendentals=0
        ),
    )(order, value)


def over_seq(value):
    count = lax.axis_size("seq")
    if count % 2:
        return lax.psum(value, "seq")
    place = lax.axis_index("seq")
    total = value
    half = count // 2
    for step in range(half - 1):
        pairs = [(step, step + 1), (count - 1 - step, count - 2 - step)]
        total = (total.astype(WIDE) + lax.ppermute(total, "seq", pairs).astype(WIDE)).astype(LOW)
    pairs = [(half - 1, half), (half, half - 1)]
    total = (total.astype(WIDE) + lax.ppermute(total, "seq", pairs).astype(WIDE)).astype(LOW)
    for step in reversed(range(half - 1)):
        pairs = [(step + 1, step), (count - 2 - step, count - 1 - step)]
        received = lax.ppermute(total, "seq", pairs)
        outside = (place == step) | (place == count - 1 - step)
        total = jnp.where(outside, received, total)
    return total


def weight_gradient(left, right):
    return jnp.einsum("nd,nf->df", left, right, preferred_element_type=WIDE)


def kept_blocks(left_ordered, right):
    half = left_ordered.shape[1] // 2
    received = moved(weight_gradient(left_ordered[:, half:], right).astype(LOW), "core")
    kept = (weight_gradient(left_ordered[:, :half], right) + received.astype(WIDE)).astype(LOW)
    return kept.reshape(4, half // 4, right.shape[1])


def kept_blocks_of_rows(term, order):
    term = term.reshape(8, -1, term.shape[-1])
    blocks = [lax.dynamic_index_in_dim(term, order[i], 0, keepdims=False) for i in range(8)]
    received = moved(jnp.stack(blocks[4:]).astype(LOW), "core")
    return [
        (blocks[i].astype(WIDE) + received[i].astype(WIDE)).astype(LOW) for i in range(4)
    ]


def scattered(members):
    own, first, second, across = (jnp.stack([m[i] for m in members]) for i in range(4))
    from_across = moved(across, 0)
    from_first = moved(first, 0)
    second = (second.astype(WIDE) + from_across.astype(WIDE)).astype(LOW)
    from_second = moved(second, 1)
    own = own.astype(WIDE) + from_first.astype(WIDE) + from_second.astype(WIDE)
    return over_seq(own.astype(LOW)).astype(WIDE)


def scattered_plainly(members):
    part = lax.psum_scatter(
        jnp.stack(members).astype(LOW), "dp", scatter_dimension=1, tiled=True
    )
    return over_seq(part).astype(WIDE)


def product(left, right):
    return jnp.dot(left, right, preferred_element_type=WIDE)


def norm_factor(value_rows):
    return lax.rsqrt(jnp.mean(value_rows * value_rows, axis=-1, keepdims=True) + EPS)


def norm_back(value_rows, factor, upstream):
    features = value_rows.shape[-1]
    inner_sum = jnp.sum(upstream * value_rows, axis=-1, keepdims=True)
    return factor * upstream - factor * factor * factor / features * value_rows * inner_sum


def local(
    hidden_in,
    mixer_weights,
    channel_in_weights,
    channel_out_weights,
    decay_rates,
    doc_lengths,
    out_cotangent,
):
    rows, tokens, features = hidden_in.shape
    heads = decay_rates.shape[1]
    head_dim = features // heads
    docs = doc_lengths.shape[1]
    count = rows * tokens
    tile = min(256, tokens)
    rates = decay_rates[0]
    start = lax.axis_index("seq") * jnp.asarray(tokens, jnp.int32)
    scalars = (start[None], rates, doc_lengths)
    ends = jnp.cumsum(doc_lengths, axis=1, dtype=jnp.int32)
    doc_before = jnp.sum((ends <= start - 1).astype(jnp.int32), axis=1)
    doc_last = jnp.sum((ends <= start + tokens - 1).astype(jnp.int32), axis=1)
    passing = jnp.where(
        (doc_before == doc_last)[:, None], jnp.exp(-rates * tokens)[None, :], 0.0
    )
    by_row = (rows, tokens, features)
    activation = jax.ShapeDtypeStruct(by_row, LOW)
    states = jax.ShapeDtypeStruct((rows, heads, head_dim, head_dim), LOW)

    by_hand = lax.axis_size("dp") == 8
    order = block_order() if by_hand else None
    scatter = scattered if by_hand else scattered_plainly

    def members(left, rights):
        if not by_hand:
            return [weight_gradient(left, right) for right in rights]
        left = ordered(left, order)
        return [kept_blocks(left, right) for right in rights]

    def gradients(left, rights):
        return scatter(members(left, rights))

    mixer = mixer_weights[0].astype(LOW)
    key_value = gathered(mixer[1:3])
    query_gate = gathered(jnp.stack([mixer[0], mixer[3]]))
    out_proj = gathered(mixer[4:5])[0]
    channel = gathered(channel_in_weights[0].astype(LOW))
    down = gathered(channel_out_weights.astype(LOW))[0]

    resid = hidden_in.astype(WIDE).reshape(count, features)
    factor_in = norm_factor(resid)
    normed = (resid * factor_in).astype(LOW)
    keys = product(normed, key_value[0]).astype(LOW).reshape(by_row)
    values = product(normed, key_value[1]).astype(LOW).reshape(by_row)
    local_state = row_call(
        functools.partial(state_kernel, docs), scalars, [keys, values], [states], [], 2 * count * features * head_dim
    )[0]
    state_in = carried(local_state, passing, tokens, 1)
    queries = product(normed, query_gate[0]).astype(LOW).reshape(by_row)
    gates = product(normed, query_gate[1]).astype(LOW).reshape(by_row)
    square = [pltpu.VMEM((tokens, tokens), WIDE)]
    part = row_call(
        functools.partial(mixing_kernel, docs, tile),
        scalars,
        [queries, keys, values],
        [activation],
        square,
        4 * count * features * tokens,
    )[0]
    mixed, gated = row_call(
        functools.partial(finish_kernel, docs),
        scalars,
        [queries, gates, part, state_in],
        [activation, activation],
        [pltpu.VMEM((tokens, features), WIDE)],
        2 * count * features * head_dim,
    )
    gated_rows = gated.reshape(count, features)
    after_mixer = resid + product(gated_rows, out_proj)
    factor_two = norm_factor(after_mixer)
    normed_two = (after_mixer * factor_two).astype(LOW)
    first = product(normed_two, channel[0]).astype(LOW)
    second = product(normed_two, channel[1]).astype(LOW)
    glu = (first.astype(WIDE) * second.astype(WIDE)).astype(LOW)
    block_output = (after_mixer + product(glu, down)).astype(LOW).reshape(by_row)

    branch = out_cotangent.reshape(count, features)
    glu_grad = jnp.einsum("nd,fd->nf", branch, down, preferred_element_type=WIDE)
    first_grad = (glu_grad * second.astype(WIDE)).astype(LOW)
    second_grad = (glu_grad * first.astype(WIDE)).astype(LOW)
    down_term = jnp.einsum("nf,nd->fd", glu, branch, preferred_element_type=WIDE)
    if by_hand:
        down_gradient = scattered([kept_blocks_of_rows(down_term.astype(LOW), order)])
    else:
        down_gradient = scattered_plainly([down_term])
    two_grad = jnp.einsum("nf,df->nd", first_grad, channel[0], preferred_element_type=WIDE)
    two_grad += jnp.einsum("nf,df->nd", second_grad, channel[1], preferred_element_type=WIDE)
    channel_gradient = gradients(normed_two, (first_grad, second_grad))
    upstream_mid = branch.astype(WIDE) + norm_back(after_mixer, factor_two, two_grad)
    middle = upstream_mid.astype(LOW)
    gated_grad = jnp.einsum("ne,de->nd", middle, out_proj, preferred_element_type=WIDE).astype(LOW)
    out_members = members(gated_rows, (middle,))
    mixed_grad, gate_grad, local_grad = row_call(
        functools.partial(back_gate_kernel, docs),
        scalars,
        [queries, gates, mixed, gated_grad.reshape(by_row)],
        [activation, activation, states],
        [],
        2 * count * features * head_dim,
    )
    state_grad = carried(local_grad, passing, tokens, -1)
    query_grad, key_part, value_part = row_call(
        functools.partial(back_mixing_kernel, docs, tile),
        scalars,
        [queries, keys, values, mixed_grad, state_in],
        [activation, activation, activation],
        square * 2,
        12 * count * features * tokens,
    )
    key_grad, value_grad = row_call(
        functools.partial(back_finish_kernel, docs),
        scalars,
        [keys, values, key_part, value_part, state_grad],
        [activation, activation],
        [],
        4 * count * features * head_dim,
    )
    grads = [
        g.reshape(count, features) for g in (query_grad, key_grad, value_grad, gate_grad)
    ]
    weights = (query_gate[0], key_value[0], key_value[1], query_gate[1])
    one_grad = sum(
        jnp.einsum("ne,de->nd", g, w, preferred_element_type=WIDE) for g, w in zip(grads, weights)
    )
    upstream = upstream_mid + norm_back(resid, factor_in, one_grad)
    outer = scatter(members(normed, grads[3:]) + out_members)
    inner = scatter(members(normed, grads[:3]))
    mixer_gradient = jnp.concatenate([inner, outer])
    return (
        block_output,
        upstream.reshape(by_row),
        mixer_gradient[None],
        channel_gradient[None],
        down_gradient,
    )


def solution(mesh):
    in_specs = (
        P("dp", "seq", None),
        P(None, None, "dp", None),
        P(None, None, "dp", None),
        P(None, "dp", None),
        P(),
        P("dp", None),
        P("dp", "seq", None),
    )
    out_specs = (
        P("dp", "seq", None),
        P("dp", "seq", None),
        P(None, None, "dp", None),
        P(None, None, "dp", None),
        P(None, "dp", None),
    )
    return jax.shard_map(local, mesh=mesh, in_specs=in_specs, out_specs=out_specs, check_vma=False)
```

```python
import functools

import jax
import jax.numpy as jnp
from jax import lax
from jax.experimental import pallas as pl
from jax.experimental.pallas import tpu as pltpu
from jax.sharding import PartitionSpec as P

EPS = 1e-06
LONGEST_DOC = 1024
LOW = jnp.bfloat16
WIDE = jnp.float32
VMEM_BYTES = 60 * 1024 * 1024
ANY = pl.BlockSpec(memory_space=pl.ANY)


def dot(left, right, left_dim=1, right_dim=0):
    return lax.dot_general(
        left, right, (((left_dim,), (right_dim,)), ((), ())), preferred_element_type=WIDE
    )


def shaped(*shape, kind=LOW):
    return jax.ShapeDtypeStruct(shape, kind)


def call(kernel, scalars, grid, inputs, in_specs, outputs, out_specs, scratch, flops):
    size = sum(a.size * a.dtype.itemsize for a in (*inputs, *outputs))
    return pl.pallas_call(
        kernel,
        out_shape=outputs,
        grid_spec=pltpu.PrefetchScalarGridSpec(
            num_scalar_prefetch=len(scalars),
            grid=grid,
            in_specs=in_specs,
            out_specs=out_specs,
            scratch_shapes=scratch,
        ),
        compiler_params=pltpu.CompilerParams(vmem_limit_bytes=VMEM_BYTES),
        cost_estimate=pl.CostEstimate(
            flops=int(flops), bytes_accessed=int(size), transcendentals=0
        ),
    )(*scalars, *inputs)


def rows_spec(tile, width):
    return pl.BlockSpec((tile, width), lambda i, *_: (i, 0))


def after(value, *others):
    return lax.optimization_barrier((value, *others))[0]


def piece_copies(order_ref, pieces, layers, columns, into_ref, sems):
    copies = []
    for index, piece in enumerate(pieces):
        rows = piece.shape[1]
        at = pl.ds(pl.multiple_of(order_ref[index] * rows, rows), rows)
        copies.append(
            pltpu.make_async_copy(
                piece.at[layers, :, columns], into_ref.at[..., at, :], sems.at[index]
            )
        )
    return copies


def started(copies):
    for copy in copies:
        copy.start()


def finished(copies):
    for copy in copies:
        copy.wait()


def doc_bounds(lengths_ref, row, docs, start, count):
    last = start + count - 1
    end = jnp.int32(0)
    last_from = jnp.int32(0)
    entry_to = jnp.int32(0)
    found = jnp.int32(0)
    for index in range(docs):
        end = end + lengths_ref[row, index]
        last_from = jnp.where(end <= last, end, last_from)
        ends_later = end > start - 1
        entry_to = jnp.where(ends_later & (found == 0), end, entry_to)
        found = jnp.where(ends_later, 1, found)
    return last_from - start, entry_to - start


def doc_starts(lengths_ref, row, docs, start, places):
    end = jnp.int32(0)
    begin = jnp.full(places.shape, -start, jnp.int32)
    for index in range(docs):
        end = end + lengths_ref[row, index]
        begin = jnp.where(places >= end - start, end - start, begin)
    return begin


def column(count, first=0):
    return first + lax.broadcasted_iota(jnp.int32, (count, 1), 0)


def project_kernel(tokens, tile, count, order_ref, h_ref, table_ref, *refs):
    pieces, (left_ref, slope_ref, right_ref, w_ref, sems) = refs[:count], refs[count:]
    step, width = pl.program_id(0), left_ref.shape[1]

    def copies(at):
        columns = pl.ds(pl.multiple_of(at * width, width), width)
        return piece_copies(
            order_ref, pieces, pl.ds(0, 2), columns, w_ref.at[at], sems.at[at]
        )

    @pl.when(step == 0)
    def _():
        for at in range(w_ref.shape[0]):
            started(copies(at))

    finished(copies(step))
    for first in range(0, h_ref.shape[0], tile):
        at = slice(first, first + tile)
        h = h_ref[at, :]
        pre = dot(h, w_ref[step, 0])
        gate = jax.nn.sigmoid(pre)
        decay = table_ref[first % tokens : first % tokens + tile, :].astype(WIDE)
        left_ref[at, :] = (pre * gate * decay).astype(LOW)
        slope_ref[at, :] = (gate * (1.0 + pre * (1.0 - gate)) * decay).astype(LOW)
        right_ref[at, :] = dot(h, w_ref[step, 1]).astype(LOW)


def project(h, table, pieces, order, tokens, tile):
    count, features = h.shape
    width = min(512, features)
    steps = features // width
    out = shaped(count, features)
    block = pl.BlockSpec((count, width), lambda i, *_: (0, i))
    return call(
        functools.partial(project_kernel, tokens, tile, len(pieces)),
        [order],
        (steps,),
        [h, table, *pieces],
        [
            pl.BlockSpec((count, features), lambda i, *_: (0, 0)),
            pl.BlockSpec((tokens, width), lambda i, *_: (0, i)),
            *[ANY] * len(pieces),
        ],
        [out] * 3,
        [block] * 3,
        [
            pltpu.VMEM((steps, 2, features, width), LOW),
            pltpu.SemaphoreType.DMA((steps, len(pieces))),
        ],
        4 * count * features * features,
    )


def state_kernel(docs, start_ref, into_ref, out_ref, lengths_ref, k_ref, v_ref, state_ref):
    count, head_dim = k_ref.shape[0], state_ref.shape[-1]
    last_from, _ = doc_bounds(lengths_ref, pl.program_id(0), docs, start_ref[0], count)
    mask = jnp.broadcast_to((column(count) >= last_from).astype(WIDE), (count, head_dim))
    for head in range(state_ref.shape[1]):
        span = slice(head * head_dim, (head + 1) * head_dim)
        keys = (k_ref[:, span].astype(WIDE) * mask).astype(LOW)
        state_ref[0, head] = (dot(keys, v_ref[:, span], 0, 0) * out_ref[head]).astype(LOW)


def mixing_kernel(
    docs, tile, heads, start_ref, into_ref, out_ref, lengths_ref, q_ref, k_ref, v_ref, o_ref, mask_ref
):
    count, features = q_ref.shape
    head_dim = features // heads
    places = column(count)
    begin = doc_starts(lengths_ref, pl.program_id(0), docs, start_ref[0], places)
    across = lax.broadcasted_iota(jnp.int32, (count, count), 1)
    mask_ref[...] = ((across <= places) & (across >= begin)).astype(WIDE)
    for head in range(heads):
        span = slice(head * head_dim, (head + 1) * head_dim)
        for first in range(0, count, tile):
            upto = first + tile
            scores = dot(q_ref[first:upto, span], k_ref[:upto, span], 1, 1)
            scores = (scores * mask_ref[first:upto, :upto]).astype(LOW)
            o_ref[first:upto, span] = dot(scores, v_ref[:upto, span]).astype(LOW)


def norm_factor(value_rows):
    return lax.rsqrt(jnp.mean(value_rows * value_rows, axis=-1, keepdims=True) + EPS)


def norm_back(value_rows, upstream):
    factor = norm_factor(value_rows)
    inner = jnp.mean(upstream * value_rows, axis=-1, keepdims=True)
    return factor * upstream - (factor * factor * factor * inner) * value_rows


def finish_kernel(
    docs,
    tokens,
    heads,
    count,
    start_ref,
    into_ref,
    out_ref,
    lengths_ref,
    order_ref,
    q_ref,
    u_ref,
    part_ref,
    x_ref,
    state_ref,
    *refs,
):
    pieces = refs[:count]
    mixed_ref, gated_ref, x1_ref, h2_ref, whole_ref, w_ref, sems = refs[count:]
    tile, features = q_ref.shape
    head_dim = features // heads
    step, steps = pl.program_id(0), tokens // tile
    layer = pieces[0].shape[0] - 1
    copies = piece_copies(order_ref, pieces, layer, pl.ds(0, features), w_ref, sems)

    @pl.when(step == 0)
    def _():
        started(copies)

    row = step // steps
    _, entry_to = doc_bounds(lengths_ref, row, docs, start_ref[0], tokens)
    mask = (column(tile, (step % steps) * tile) < entry_to).astype(WIDE)
    mask = jnp.broadcast_to(mask, (tile, head_dim))
    for head in range(heads):
        span = slice(head * head_dim, (head + 1) * head_dim)
        state = (state_ref[0, head].astype(WIDE) * into_ref[head]).astype(LOW)
        whole_ref[:, span] = part_ref[:, span].astype(WIDE) + dot(q_ref[:, span], state) * mask
    mixed = whole_ref[...]
    mixed_ref[...] = mixed.astype(LOW)
    gated = (mixed * norm_factor(mixed) * u_ref[...].astype(WIDE)).astype(LOW)
    gated_ref[...] = gated

    @pl.when(step == 0)
    def _():
        finished(copies)

    x1 = x_ref[...].astype(WIDE) + dot(gated, w_ref[...])
    x1_ref[...] = x1.astype(LOW)
    h2_ref[...] = (x1 * norm_factor(x1)).astype(LOW)


def pair_kernel(tile, count, order_ref, h_ref, *refs):
    pieces, (first_ref, second_ref, turned_ref, w_ref, sems) = refs[:count], refs[count:]
    step, width = pl.program_id(0), first_ref.shape[1]

    def copies(at):
        columns = pl.ds(pl.multiple_of(at * width, 128), width)
        return piece_copies(
            order_ref, pieces, pl.ds(0, 2), columns, w_ref.at[at], sems.at[at]
        )

    @pl.when(step == 0)
    def _():
        for at in range(w_ref.shape[0]):
            started(copies(at))

    finished(copies(step))
    for begin in range(0, h_ref.shape[0], tile):
        at = slice(begin, begin + tile)
        h = h_ref[at, :]
        first = dot(h, w_ref[step, 0])
        second = dot(h, w_ref[step, 1])
        first_ref[at, :] = first.astype(LOW)
        second_ref[at, :] = second.astype(LOW)
        turned_ref[:, at] = (first * second).astype(LOW).T


def pair(h, pieces, order, tile):
    (count, features), hidden = h.shape, pieces[0].shape[-1]
    steps = 2 if hidden % 256 == 0 else 1
    width = hidden // steps
    block = pl.BlockSpec((count, width), lambda i, *_: (0, i))
    return call(
        functools.partial(pair_kernel, tile, len(pieces)),
        [order],
        (steps,),
        [h, *pieces],
        [pl.BlockSpec((count, features), lambda i, *_: (0, 0)), *[ANY] * len(pieces)],
        [shaped(count, hidden), shaped(count, hidden), shaped(hidden, count)],
        [block, block, pl.BlockSpec((width, count), lambda i, *_: (i, 0))],
        [
            pltpu.VMEM((steps, 2, features, width), LOW),
            pltpu.SemaphoreType.DMA((steps, len(pieces))),
        ],
        4 * count * features * hidden,
    )


def down_kernel(count, order_ref, first_ref, second_ref, x1_ref, dy_ref, *refs):
    pieces, (y_ref, dpair_ref, w_ref, sems) = refs[:count], refs[count:]
    copies = piece_copies(order_ref, pieces, 0, pl.ds(0, w_ref.shape[1]), w_ref, sems)

    @pl.when(pl.program_id(0) == 0)
    def _():
        started(copies)
        finished(copies)

    grad = dot(dy_ref[...], w_ref[...], 1, 1)
    dpair_ref[0] = (grad * second_ref[...].astype(WIDE)).astype(LOW)
    dpair_ref[1] = (grad * first_ref[...].astype(WIDE)).astype(LOW)
    glu = (first_ref[...].astype(WIDE) * second_ref[...].astype(WIDE)).astype(LOW)
    y_ref[...] = (x1_ref[...].astype(WIDE) + dot(glu, w_ref[...])).astype(LOW)


def down_and_back(first, second, x1, dy, pieces, order, tile):
    (count, hidden), features = first.shape, x1.shape[1]
    wide, narrow = rows_spec(tile, hidden), rows_spec(tile, features)
    return call(
        functools.partial(down_kernel, len(pieces)),
        [order],
        (count // tile,),
        [first, second, x1, dy, *pieces],
        [wide, wide, narrow, narrow, *[ANY] * len(pieces)],
        [shaped(count, features), shaped(2, count, hidden)],
        [narrow, pl.BlockSpec((2, tile, hidden), lambda i, *_: (0, i, 0))],
        [pltpu.VMEM((hidden, features), LOW), pltpu.SemaphoreType.DMA((len(pieces),))],
        4 * count * features * hidden,
    )


def pair_back_kernel(count, order_ref, dpair_ref, x1_ref, dy_ref, *refs):
    pieces, (e1_ref, w_ref, sems) = refs[:count], refs[count:]
    step = pl.program_id(0)

    def copies(layer):
        return piece_copies(
            order_ref, pieces, layer, pl.ds(0, w_ref.shape[2]), w_ref.at[layer], sems.at[layer]
        )

    @pl.when(step == 0)
    def _():
        started(copies(0))
        started(copies(1))
        finished(copies(0))

    total = dot(dpair_ref[0], w_ref[0], 1, 1)

    @pl.when(step == 0)
    def _():
        finished(copies(1))

    total = total + dot(dpair_ref[1], w_ref[1], 1, 1)
    e1 = dy_ref[...].astype(WIDE) + norm_back(x1_ref[...].astype(WIDE), total)
    e1_ref[...] = e1.astype(LOW)


def pair_back(dpair, x1, dy, pieces, order, tile):
    (_, count, hidden), features = dpair.shape, x1.shape[1]
    narrow = rows_spec(tile, features)
    return call(
        functools.partial(pair_back_kernel, len(pieces)),
        [order],
        (count // tile,),
        [dpair, x1, dy, *pieces],
        [
            pl.BlockSpec((2, tile, hidden), lambda i, *_: (0, i, 0)),
            narrow,
            narrow,
            *[ANY] * len(pieces),
        ],
        [shaped(count, features)],
        [narrow],
        [pltpu.VMEM((2, features, hidden), LOW), pltpu.SemaphoreType.DMA((2, len(pieces)))],
        4 * count * features * hidden,
    )[0]


def back_gate_kernel(
    docs,
    heads,
    count,
    start_ref,
    into_ref,
    out_ref,
    lengths_ref,
    order_ref,
    e1_ref,
    q_ref,
    u_ref,
    mixed_ref,
    *refs,
):
    pieces, (dmixed_ref, du_ref, grad_ref, w_ref, sems) = refs[:count], refs[count:]
    tokens, features = q_ref.shape
    head_dim = features // heads
    layer = pieces[0].shape[0] - 1
    copies = piece_copies(order_ref, pieces, layer, pl.ds(0, features), w_ref, sems)

    @pl.when(pl.program_id(0) == 0)
    def _():
        started(copies)
        finished(copies)

    dgated = dot(e1_ref[...], w_ref[...], 1, 1)
    mixed = mixed_ref[...].astype(WIDE)
    du_ref[...] = (dgated * (mixed * norm_factor(mixed))).astype(LOW)
    dmixed_ref[...] = norm_back(mixed, dgated * u_ref[...].astype(WIDE)).astype(LOW)
    _, entry_to = doc_bounds(lengths_ref, pl.program_id(0), docs, start_ref[0], tokens)
    mask = jnp.broadcast_to((column(tokens) < entry_to).astype(WIDE), (tokens, head_dim))
    for head in range(heads):
        span = slice(head * head_dim, (head + 1) * head_dim)
        queries = (q_ref[:, span].astype(WIDE) * mask).astype(LOW)
        grad_ref[0, head] = (dot(queries, dmixed_ref[:, span], 0, 0) * into_ref[head]).astype(LOW)


def back_mixing_kernel(
    docs,
    tile,
    heads,
    start_ref,
    into_ref,
    out_ref,
    lengths_ref,
    q_ref,
    slope_ref,
    k_ref,
    v_ref,
    dmixed_ref,
    state_ref,
    dq_ref,
    dk_ref,
    dv_ref,
    mask_ref,
    turned_ref,
):
    count, features = q_ref.shape
    head_dim = features // heads
    row, start = pl.program_id(0), start_ref[0]
    _, entry_to = doc_bounds(lengths_ref, row, docs, start, count)
    places = column(count)
    begin = doc_starts(lengths_ref, row, docs, start, places)
    across = lax.broadcasted_iota(jnp.int32, (count, count), 1)
    mask_ref[...] = ((across <= places) & (across >= begin)).astype(WIDE)
    flat = lax.broadcasted_iota(jnp.int32, (1, count), 1)
    begin = doc_starts(lengths_ref, row, docs, start, flat)
    down = lax.broadcasted_iota(jnp.int32, (count, count), 0)
    turned_ref[...] = ((down <= flat) & (down >= begin)).astype(WIDE)
    entry = jnp.broadcast_to((places < entry_to).astype(WIDE), (count, head_dim))
    for head in range(heads):
        span = slice(head * head_dim, (head + 1) * head_dim)
        state = (state_ref[0, head].astype(WIDE) * into_ref[head]).astype(LOW)
        for first in range(0, count, tile):
            upto = first + tile
            here = slice(first, upto)
            grads = dot(dmixed_ref[here, span], v_ref[:upto, span], 1, 1)
            dq = dot((grads * mask_ref[here, :upto]).astype(LOW), k_ref[:upto, span])
            dq = dq + dot(dmixed_ref[here, span], state, 1, 1) * entry[here]
            dq_ref[here, span] = (dq * slope_ref[here, span].astype(WIDE)).astype(LOW)
            turned = turned_ref[here, first:]
            grads = dot(v_ref[here, span], dmixed_ref[first:, span], 1, 1) * turned
            dk_ref[here, span] = dot(grads.astype(LOW), q_ref[first:, span]).astype(LOW)
            scores = dot(k_ref[here, span], q_ref[first:, span], 1, 1) * turned
            dv_ref[here, span] = dot(scores.astype(LOW), dmixed_ref[first:, span]).astype(LOW)


def back_finish_kernel(
    docs,
    heads,
    start_ref,
    into_ref,
    out_ref,
    lengths_ref,
    k_ref,
    slope_ref,
    v_ref,
    dk_part_ref,
    dv_part_ref,
    grad_ref,
    dk_ref,
    dv_ref,
):
    count, features = k_ref.shape
    head_dim = features // heads
    last_from, _ = doc_bounds(lengths_ref, pl.program_id(0), docs, start_ref[0], count)
    mask = jnp.broadcast_to((column(count) >= last_from).astype(WIDE), (count, head_dim))
    for head in range(heads):
        span = slice(head * head_dim, (head + 1) * head_dim)
        grad = (grad_ref[0, head].astype(WIDE) * out_ref[head]).astype(LOW)
        dk = dot(v_ref[:, span], grad, 1, 1) * mask + dk_part_ref[:, span].astype(WIDE)
        dk_ref[:, span] = (dk * slope_ref[:, span].astype(WIDE)).astype(LOW)
        dv = dot(k_ref[:, span], grad) * mask + dv_part_ref[:, span].astype(WIDE)
        dv_ref[:, span] = dv.astype(LOW)


def mixer_back_kernel(counts, order_ref, dq_ref, dk_ref, dv_ref, du_ref, x_ref, e1_ref, *refs):
    total = sum(counts)
    pieces, (out_ref, w_ref, sems) = refs[:total], refs[total:]
    groups = (pieces[: counts[0]], pieces[counts[0] :])
    grads = ((dk_ref, 0, 0), (dv_ref, 0, 1), (dq_ref, 1, 0), (du_ref, 1, 1))
    step, features = pl.program_id(0), x_ref.shape[1]

    def copies(index):
        _, group, layer = grads[index]
        return piece_copies(
            order_ref, groups[group], layer, pl.ds(0, features), w_ref.at[index], sems.at[index]
        )

    @pl.when(step == 0)
    def _():
        for index in range(4):
            started(copies(index))

    total = None
    for index in range(4):

        @pl.when(step == 0)
        def _(index=index):
            finished(copies(index))

        term = dot(grads[index][0][...], w_ref[index], 1, 1)
        total = term if total is None else total + term
    out_ref[...] = e1_ref[...].astype(WIDE) + norm_back(x_ref[...].astype(WIDE), total)


def mixer_back(grads, x, e1, key_value, rest, order, tile):
    count, features = x.shape
    spec = rows_spec(tile, features)
    pieces = [*key_value, *rest]
    return call(
        functools.partial(mixer_back_kernel, (len(key_value), len(rest))),
        [order],
        (count // tile,),
        [*grads, x, e1, *pieces],
        [spec] * 6 + [ANY] * len(pieces),
        [shaped(count, features, kind=WIDE)],
        [spec],
        [
            pltpu.VMEM((4, features, features), LOW),
            pltpu.SemaphoreType.DMA((4, len(key_value))),
        ],
        8 * count * features * features,
    )[0]


def block_grads_kernel(layers, received, order_ref, *refs):
    members = len(layers)
    left_ref, rights, refs = refs[0], refs[1 : 1 + members], refs[1 + members :]
    if received:
        add_ref, *refs = refs
    *out_refs, blocks_ref, turned_ref, right_ref, left_sems, sems = refs
    member, at = pl.program_id(0), pl.program_id(1)
    tiles, width, tile = blocks_ref.shape[0], blocks_ref.shape[2], right_ref.shape[-1]
    steps = right_ref.shape[1]

    def left_copy(index):
        columns = pl.ds(pl.multiple_of(order_ref[index] * width, width), width)
        return pltpu.make_async_copy(
            left_ref.at[:, columns], blocks_ref.at[index], left_sems.at[index]
        )

    def right_copy(index, step):
        right = rights[index] if layers[index] is None else rights[index].at[layers[index]]
        return pltpu.make_async_copy(
            right.at[:, pl.ds(pl.multiple_of(step * tile, 128), tile)],
            right_ref.at[index, step],
            sems.at[index, step],
        )

    @pl.when((member == 0) & (at == 0))
    def _():
        for index in range(tiles):
            left_copy(index).start()
        for index in range(members):
            for step in range(steps):
                right_copy(index, step).start()
        for index in range(tiles):
            left_copy(index).wait()
            turned_ref[index * width : (index + 1) * width, :] = blocks_ref[index].T

    for index in range(members):

        @pl.when(member == index)
        def _(index=index):
            right_copy(index, at).wait()

    term = dot(turned_ref[...], right_ref[member, at])
    if received:
        term = (term + add_ref[0].astype(WIDE)).astype(LOW)
        for index, out_ref in enumerate(out_refs):
            out_ref[0] = term[index * width : (index + 1) * width]
    else:
        out_refs[0][0] = term.astype(LOW)


def block_grads(left, rights, order, received=None):
    (count, features), columns = left.shape, rights[0][0].shape[-1]
    width, blocks = features // 8, order.shape[0]
    steps = 2 if columns % 256 == 0 and columns > 1024 else 1
    tile, members = columns // steps, len(rights)

    def spec(height):
        return pl.BlockSpec((1, height, tile), lambda i, j, *_: (i, 0, j))

    whole = blocks * width
    outputs, height, extra = 1, whole, []
    if received is not None:
        outputs, height, extra = blocks, width, [received]
    results = call(
        functools.partial(block_grads_kernel, [layer for _, layer in rights], bool(extra)),
        [order],
        (members, steps),
        [left, *(right for right, _ in rights), *extra],
        [ANY] * (1 + members) + [spec(whole)] * len(extra),
        [shaped(members, height, columns)] * outputs,
        [spec(height)] * outputs,
        [
            pltpu.VMEM((blocks, count, width), LOW),
            pltpu.VMEM((whole, count), LOW),
            pltpu.VMEM((members, steps, count, tile), LOW),
            pltpu.SemaphoreType.DMA((blocks,)),
            pltpu.SemaphoreType.DMA((members, steps)),
        ],
        2 * members * count * whole * columns,
    )
    return results if extra else results[0]


def row_grads_kernel(half, order_ref, turned_ref, right_ref, send_ref, keep_ref):
    step = pl.program_id(0)
    term = dot(turned_ref[...], right_ref[...]).astype(LOW)

    @pl.when(step < half)
    def _():
        send_ref[0] = term

    @pl.when(step >= half)
    def _():
        keep_ref[0] = term


def row_grads(turned, right, order):
    (hidden, count), columns = turned.shape, right.shape[1]
    blocks = order.shape[0]
    half, width = blocks // 2, hidden // blocks
    out = shaped(half, width, columns)
    return call(
        functools.partial(row_grads_kernel, half),
        [order],
        (blocks,),
        [turned, right],
        [
            pl.BlockSpec((width, count), lambda i, order: (order[(i + half) % blocks], 0)),
            pl.BlockSpec((count, columns), lambda i, *_: (0, 0)),
        ],
        [out, out],
        [
            pl.BlockSpec((1, width, columns), lambda i, *_: (jnp.minimum(i, half - 1), 0, 0)),
            pl.BlockSpec((1, width, columns), lambda i, *_: (jnp.maximum(i - half, 0), 0, 0)),
        ],
        [],
        2 * hidden * count * columns,
    )


def passed_along(value, steps):
    count = lax.axis_size("seq")
    leading, last = max(0, -steps), min(count, count - steps)
    return lax.ppermute(value, "seq", [(source, source + steps) for source in range(leading, last)])


def hops_needed(tokens):
    return min((LONGEST_DOC - 2) // tokens + 1, lax.axis_size("seq") - 1)


def carried(local_state, passing, tokens, steps, between=()):
    message, total, ran = local_state, None, []
    for hop in range(hops_needed(tokens)):
        received = passed_along(message, steps)
        if hop < len(between):
            ran.append(between[hop]())
            received = after(received, *jax.tree.leaves(ran[-1]))
        total = received.astype(WIDE) if total is None else total + received.astype(WIDE)
        message = (passing[..., None, None] * received.astype(WIDE)).astype(LOW)
    return total.astype(LOW), ran


def side_steps(device):
    return (2, 4) if device % 2 == 0 else (4, 2)


def moved(value, kind):
    count = lax.axis_size("dp")
    if kind == "core":
        pairs = [(device, device ^ 1) for device in range(count)]
    else:
        pairs = [(device, device ^ side_steps(device)[kind]) for device in range(count)]
    return lax.ppermute(value, "dp", pairs)


def block_order():
    device = lax.axis_index("dp")
    table = []
    for index in range(8):
        row = []
        for mine in (index, index ^ 1):
            first, second = side_steps(mine)
            row += [mine, mine ^ first, mine ^ second, mine ^ first ^ second]
        table.append(row)
    return jnp.asarray(table, jnp.int32)[device]


def gathered(piece):
    first, second = moved(piece, 0), moved(piece, 1)
    mine = [piece, first, second, moved(first, 1)]
    return mine + [moved(part, "core") for part in mine], (first, second)


def over_seq(value):
    count = lax.axis_size("seq")
    if count % 2:
        return lax.psum(value, "seq")
    place = lax.axis_index("seq")
    total = value
    half = count // 2
    for step in range(half - 1):
        pairs = [(step, step + 1), (count - 1 - step, count - 2 - step)]
        total = (total.astype(WIDE) + lax.ppermute(total, "seq", pairs).astype(WIDE)).astype(LOW)
    pairs = [(half - 1, half), (half, half - 1)]
    total = (total.astype(WIDE) + lax.ppermute(total, "seq", pairs).astype(WIDE)).astype(LOW)
    for step in reversed(range(half - 1)):
        pairs = [(step + 1, step), (count - 2 - step, count - 1 - step)]
        received = lax.ppermute(total, "seq", pairs)
        outside = (place == step) | (place == count - 1 - step)
        total = jnp.where(outside, received, total)
    return total


def plus(*terms):
    return sum(term.astype(WIDE) for term in terms).astype(LOW)


def scattered(own, first, second, across):
    from_across = moved(across, 0)
    from_first = moved(first, 0)
    from_second = moved(plus(second, from_across), 1)
    return over_seq(plus(own, from_first, from_second)).astype(WIDE)


def scattered_plainly(left, rights):
    terms = [
        lax.dot_general(left, right, (((0,), (0,)), ((), ())), preferred_element_type=WIDE)
        for right in rights
    ]
    part = lax.psum_scatter(jnp.stack(terms).astype(LOW), "dp", scatter_dimension=1, tiled=True)
    return over_seq(part).astype(WIDE)


def local(
    hidden_in,
    mixer_weights,
    channel_in_weights,
    channel_out_weights,
    decay_rates,
    doc_lengths,
    out_cotangent,
):
    rows, tokens, features = hidden_in.shape
    heads = decay_rates.shape[1]
    head_dim = features // heads
    docs = doc_lengths.shape[1]
    count = rows * tokens
    tile = min(256, tokens)
    by_hand = lax.axis_size("dp") == 8
    order = block_order() if by_hand else jnp.zeros((1,), jnp.int32)
    rates = decay_rates[0]
    start = lax.axis_index("seq") * jnp.asarray(tokens, jnp.int32)
    centre = tokens // 2
    into = jnp.exp(-rates * (centre + 1))
    out = jnp.exp(-rates * (tokens - 1 - centre))
    scalars = [start[None], into, out, doc_lengths]
    ends = jnp.cumsum(doc_lengths, axis=1, dtype=jnp.int32)
    doc_before = jnp.sum((ends <= start - 1).astype(jnp.int32), axis=1)
    doc_last = jnp.sum((ends <= start + tokens - 1).astype(jnp.int32), axis=1)
    passing = jnp.where(
        (doc_before == doc_last)[:, None], jnp.exp(-rates * tokens)[None, :], 0.0
    )
    centred = (jnp.arange(tokens, dtype=jnp.int32) - centre).astype(WIDE)[:, None]
    spread = jnp.repeat(rates, head_dim)[None, :] * centred
    query_table, key_table = jnp.exp(-spread), jnp.exp(spread)

    def gather(piece, *others):
        if not by_hand:
            return [lax.all_gather(piece, "dp", axis=1, tiled=True)], ()
        return gathered(after(piece, *others) if others else piece)

    mixer = mixer_weights[0]
    key_value, arrived = gather(mixer[1:3].astype(LOW))
    rest = jnp.stack([mixer[0], mixer[3], mixer[4]]).astype(LOW)
    rest, arrived = gather(rest, *arrived)
    channel, arrived = gather(channel_in_weights[0].astype(LOW), *arrived)
    down, arrived = gather(channel_out_weights.astype(LOW), *arrived)

    x = hidden_in.reshape(count, features)
    wide_x = x.astype(WIDE)
    h = (wide_x * norm_factor(wide_x)).astype(LOW)
    dy = out_cotangent.reshape(count, features)
    narrow = shaped(count, features)
    states = shaped(rows, heads, head_dim, head_dim)
    row_spec = rows_spec(tokens, features)
    state_spec = pl.BlockSpec((1, heads, head_dim, head_dim), lambda i, *_: (i, 0, 0, 0))
    square = pltpu.VMEM((tokens, tokens), WIDE)

    k, k_slope, v = project(h, key_table, key_value, order, tokens, tile)
    local_state = call(
        functools.partial(state_kernel, docs),
        scalars,
        (rows,),
        [k, v],
        [row_spec] * 2,
        [states],
        [state_spec],
        [],
        2 * count * features * head_dim,
    )[0]

    def inside():
        q, q_slope, u = project(after(h, local_state), query_table, rest, order, tokens, tile)
        part = call(
            functools.partial(mixing_kernel, docs, tile, heads),
            scalars,
            (rows,),
            [q, k, v],
            [row_spec] * 3,
            [narrow],
            [row_spec],
            [square],
            4 * count * features * tokens,
        )[0]
        return q, q_slope, u, part

    state_in, _ = carried(local_state, passing, tokens, 1)
    q, q_slope, u, part = inside()
    spec = rows_spec(tile, features)
    steps = tokens // tile
    mixed, gated, x1, h2 = call(
        functools.partial(finish_kernel, docs, tokens, heads, len(rest)),
        [*scalars, order],
        (count // tile,),
        [q, u, part, x, state_in, *rest],
        [spec] * 4
        + [
            pl.BlockSpec(
                (1, heads, head_dim, head_dim), lambda i, *_: (i // steps, 0, 0, 0)
            )
        ]
        + [ANY] * len(rest),
        [narrow] * 4,
        [spec] * 4,
        [
            pltpu.VMEM((tile, features), WIDE),
            pltpu.VMEM((features, features), LOW),
            pltpu.SemaphoreType.DMA((len(rest),)),
        ],
        2 * count * features * (features + head_dim),
    )
    first, second, turned = pair(h2, channel, order, tile)
    if by_hand:
        send_down, keep_down = row_grads(turned, dy, order)
        received_down = moved(send_down, "core")
        keep_down = [plus(keep_down[i], received_down[i])[None] for i in range(4)]
        down_gradient = scattered(*keep_down)
        first = after(first, send_down)
    else:
        down_gradient = scattered_plainly(turned.T, [dy])
    y, dpair = down_and_back(first, second, x1, dy, down, order, tile)

    if by_hand:
        sent = block_grads(h2, [(dpair, 0), (dpair, 1)], order[4:])
        received = moved(sent, "core")
        e1 = pair_back(after(dpair, sent), x1, dy, channel, order, tile)
    else:
        channel_gradient = scattered_plainly(h2, [dpair[0], dpair[1]])
        e1 = pair_back(dpair, x1, dy, channel, order, tile)
    dmixed, du, local_grad = call(
        functools.partial(back_gate_kernel, docs, heads, len(rest)),
        [*scalars, order],
        (rows,),
        [e1, q, u, mixed, *rest],
        [row_spec] * 4 + [ANY] * len(rest),
        [narrow, narrow, states],
        [row_spec, row_spec, state_spec],
        [pltpu.VMEM((features, features), LOW), pltpu.SemaphoreType.DMA((len(rest),))],
        2 * count * features * (features + head_dim),
    )

    def back_inside(*others):
        return call(
            functools.partial(back_mixing_kernel, docs, tile, heads),
            scalars,
            (rows,),
            [q, q_slope, k, v, after(dmixed, *others), state_in],
            [row_spec] * 5 + [state_spec],
            [narrow] * 3,
            [row_spec] * 3,
            [square] * 2,
            12 * count * features * tokens,
        )

    if by_hand:

        def channel_kept():
            own = after(h2, local_grad)
            return block_grads(own, [(dpair, 0), (dpair, 1)], order[:4], received)

        def inner():
            return back_inside(*kept[0])

        kept = []

        def outer():
            sent_o = block_grads(after(gated, local_grad), [(e1, None)], order[4:])
            kept.append(channel_kept())
            return sent_o, kept[0]

        state_grad, ((sent_o, _), (dq, dk_part, dv_part)) = carried(
            local_grad, passing, tokens, -1, (outer, inner)
        )
        channel_gradient = scattered(*kept[0])
        received_o = moved(sent_o, "core")
        sent_uq = block_grads(after(h, dq), [(du, None), (dq, None)], order[4:])
        received_uq = moved(sent_uq, "core")
    else:
        dq, dk_part, dv_part = back_inside()
        state_grad, _ = carried(local_grad, passing, tokens, -1)
        sent_uq = dq
    dk, dv = call(
        functools.partial(back_finish_kernel, docs, heads),
        scalars,
        (rows,),
        [k, k_slope, v, after(dk_part, sent_uq), dv_part, state_grad],
        [row_spec] * 5 + [state_spec],
        [narrow] * 2,
        [row_spec] * 2,
        [],
        4 * count * features * head_dim,
    )
    grads = [dq, dk, dv, du]
    if by_hand:
        sent_kv = block_grads(h, [(dk, None), (dv, None)], order[4:])
        received_kv = moved(sent_kv, "core")
        kept_o = block_grads(after(gated, sent_kv), [(e1, None)], order[:4], received_o)
        kept_uq = block_grads(
            after(h, sent_kv), [(du, None), (dq, None)], order[:4], received_uq
        )
        kept_kv = block_grads(
            after(h, *kept_o, *kept_uq), [(dk, None), (dv, None)], order[:4], received_kv
        )
        outer_gradient = scattered(
            *(jnp.concatenate([a, b]) for a, b in zip(kept_uq, kept_o))
        )
        inner_gradient = scattered(*kept_kv)
        mixer_gradient = jnp.stack(
            [
                outer_gradient[1],
                inner_gradient[0],
                inner_gradient[1],
                outer_gradient[0],
                outer_gradient[2],
            ]
        )
        grads[0] = after(dq, *kept_kv)
    else:
        mixer_gradient = jnp.concatenate(
            [scattered_plainly(h, grads), scattered_plainly(gated, [e1])]
        )
    upstream = mixer_back(grads, x, e1, key_value, rest, order, tile)
    by_row = (rows, tokens, features)
    return (
        y.reshape(by_row),
        upstream.reshape(by_row),
        mixer_gradient[None],
        channel_gradient[None],
        down_gradient,
    )


def solution(mesh):
    in_specs = (
        P("dp", "seq", None),
        P(None, None, "dp", None),
        P(None, None, "dp", None),
        P(None, "dp", None),
        P(),
        P("dp", None),
        P("dp", "seq", None),
    )
    out_specs = (
        P("dp", "seq", None),
        P("dp", "seq", None),
        P(None, None, "dp", None),
        P(None, None, "dp", None),
        P(None, "dp", None),
    )
    return jax.shard_map(local, mesh=mesh, in_specs=in_specs, out_specs=out_specs, check_vma=False)
```

```python
import functools

import jax
import jax.numpy as jnp
from jax import lax
from jax.experimental import pallas as pl
from jax.experimental.pallas import tpu as pltpu
from jax.sharding import PartitionSpec as P

EPS = 1e-06
LONGEST_DOC = 1024
LOW = jnp.bfloat16
WIDE = jnp.float32
VMEM_BYTES = 60 * 1024 * 1024
ANY = pl.BlockSpec(memory_space=pl.ANY)


def dot(left, right, left_dim=1, right_dim=0):
    return lax.dot_general(
        left, right, (((left_dim,), (right_dim,)), ((), ())), preferred_element_type=WIDE
    )


def shaped(*shape, kind=LOW):
    return jax.ShapeDtypeStruct(shape, kind)


def call(kernel, scalars, grid, inputs, in_specs, outputs, out_specs, scratch, flops):
    size = sum(a.size * a.dtype.itemsize for a in (*inputs, *outputs))
    return pl.pallas_call(
        kernel,
        out_shape=outputs,
        grid_spec=pltpu.PrefetchScalarGridSpec(
            num_scalar_prefetch=len(scalars),
            grid=grid,
            in_specs=in_specs,
            out_specs=out_specs,
            scratch_shapes=scratch,
        ),
        compiler_params=pltpu.CompilerParams(vmem_limit_bytes=VMEM_BYTES),
        cost_estimate=pl.CostEstimate(
            flops=int(flops), bytes_accessed=int(size), transcendentals=0
        ),
    )(*scalars, *inputs)


def rows_spec(tile, width):
    return pl.BlockSpec((tile, width), lambda i, *_: (i, 0))


def after(value, *others):
    return lax.optimization_barrier((value, *others))[0]


def piece_copies(order_ref, pieces, layers, columns, into_ref, sems):
    copies = []
    for index, piece in enumerate(pieces):
        rows = piece.shape[1]
        at = pl.ds(pl.multiple_of(order_ref[index] * rows, rows), rows)
        copies.append(
            pltpu.make_async_copy(
                piece.at[layers, :, columns], into_ref.at[..., at, :], sems.at[index]
            )
        )
    return copies


def started(copies):
    for copy in copies:
        copy.start()


def finished(copies):
    for copy in copies:
        copy.wait()


def doc_bounds(lengths_ref, row, docs, start, count):
    last = start + count - 1
    end = jnp.int32(0)
    last_from = jnp.int32(0)
    entry_to = jnp.int32(0)
    found = jnp.int32(0)
    for index in range(docs):
        end = end + lengths_ref[row, index]
        last_from = jnp.where(end <= last, end, last_from)
        ends_later = end > start - 1
        entry_to = jnp.where(ends_later & (found == 0), end, entry_to)
        found = jnp.where(ends_later, 1, found)
    return last_from - start, entry_to - start


def doc_starts(lengths_ref, row, docs, start, places):
    end = jnp.int32(0)
    begin = jnp.full(places.shape, -start, jnp.int32)
    for index in range(docs):
        end = end + lengths_ref[row, index]
        begin = jnp.where(places >= end - start, end - start, begin)
    return begin


def column(count, first=0):
    return first + lax.broadcasted_iota(jnp.int32, (count, 1), 0)


def project_kernel(tokens, tile, count, order_ref, h_ref, table_ref, *refs):
    pieces, (left_ref, slope_ref, right_ref, w_ref, sems) = refs[:count], refs[count:]
    step, width = pl.program_id(0), left_ref.shape[1]

    def copies(at):
        columns = pl.ds(pl.multiple_of(at * width, width), width)
        return piece_copies(
            order_ref, pieces, pl.ds(0, 2), columns, w_ref.at[at], sems.at[at]
        )

    @pl.when(step == 0)
    def _():
        for at in range(w_ref.shape[0]):
            started(copies(at))

    finished(copies(step))
    for first in range(0, h_ref.shape[0], tile):
        at = slice(first, first + tile)
        h = h_ref[at, :]
        pre = dot(h, w_ref[step, 0])
        gate = jax.nn.sigmoid(pre)
        decay = table_ref[first % tokens : first % tokens + tile, :].astype(WIDE)
        left_ref[at, :] = (pre * gate * decay).astype(LOW)
        slope_ref[at, :] = (gate * (1.0 + pre * (1.0 - gate)) * decay).astype(LOW)
        right_ref[at, :] = dot(h, w_ref[step, 1]).astype(LOW)


def project(h, table, pieces, order, tokens, tile):
    count, features = h.shape
    width = min(512, features)
    steps = features // width
    out = shaped(count, features)
    block = pl.BlockSpec((count, width), lambda i, *_: (0, i))
    return call(
        functools.partial(project_kernel, tokens, tile, len(pieces)),
        [order],
        (steps,),
        [h, table, *pieces],
        [
            pl.BlockSpec((count, features), lambda i, *_: (0, 0)),
            pl.BlockSpec((tokens, width), lambda i, *_: (0, i)),
            *[ANY] * len(pieces),
        ],
        [out] * 3,
        [block] * 3,
        [
            pltpu.VMEM((steps, 2, features, width), LOW),
            pltpu.SemaphoreType.DMA((steps, len(pieces))),
        ],
        4 * count * features * features,
    )


def state_kernel(docs, start_ref, into_ref, out_ref, lengths_ref, k_ref, v_ref, state_ref):
    count, head_dim = k_ref.shape[0], state_ref.shape[-1]
    last_from, _ = doc_bounds(lengths_ref, pl.program_id(0), docs, start_ref[0], count)
    mask = jnp.broadcast_to((column(count) >= last_from).astype(WIDE), (count, head_dim))
    for head in range(state_ref.shape[1]):
        span = slice(head * head_dim, (head + 1) * head_dim)
        keys = (k_ref[:, span].astype(WIDE) * mask).astype(LOW)
        state_ref[0, head] = (dot(keys, v_ref[:, span], 0, 0) * out_ref[head]).astype(LOW)


def mixing_kernel(
    docs, tile, heads, start_ref, into_ref, out_ref, lengths_ref, q_ref, k_ref, v_ref, o_ref, mask_ref
):
    count, features = q_ref.shape
    head_dim = features // heads
    places = column(count)
    begin = doc_starts(lengths_ref, pl.program_id(0), docs, start_ref[0], places)
    across = lax.broadcasted_iota(jnp.int32, (count, count), 1)
    mask_ref[...] = ((across <= places) & (across >= begin)).astype(WIDE)
    for head in range(heads):
        span = slice(head * head_dim, (head + 1) * head_dim)
        for first in range(0, count, tile):
            upto = first + tile
            scores = dot(q_ref[first:upto, span], k_ref[:upto, span], 1, 1)
            scores = (scores * mask_ref[first:upto, :upto]).astype(LOW)
            o_ref[first:upto, span] = dot(scores, v_ref[:upto, span]).astype(LOW)


def norm_factor(value_rows):
    return lax.rsqrt(jnp.mean(value_rows * value_rows, axis=-1, keepdims=True) + EPS)


def norm_back(value_rows, upstream):
    factor = norm_factor(value_rows)
    inner = jnp.mean(upstream * value_rows, axis=-1, keepdims=True)
    return factor * upstream - (factor * factor * factor * inner) * value_rows


def finish_kernel(
    docs,
    tokens,
    heads,
    count,
    start_ref,
    into_ref,
    out_ref,
    lengths_ref,
    order_ref,
    q_ref,
    u_ref,
    part_ref,
    x_ref,
    state_ref,
    *refs,
):
    pieces = refs[:count]
    mixed_ref, gated_ref, x1_ref, h2_ref, h2_turned_ref, whole_ref, w_ref, sems = refs[count:]
    tile, features = q_ref.shape
    head_dim = features // heads
    step, steps = pl.program_id(0), tokens // tile
    layer = pieces[0].shape[0] - 1
    copies = piece_copies(order_ref, pieces, layer, pl.ds(0, features), w_ref, sems)

    @pl.when(step == 0)
    def _():
        started(copies)

    row = step // steps
    _, entry_to = doc_bounds(lengths_ref, row, docs, start_ref[0], tokens)
    mask = (column(tile, (step % steps) * tile) < entry_to).astype(WIDE)
    mask = jnp.broadcast_to(mask, (tile, head_dim))
    for head in range(heads):
        span = slice(head * head_dim, (head + 1) * head_dim)
        state = (state_ref[0, head].astype(WIDE) * into_ref[head]).astype(LOW)
        whole_ref[:, span] = part_ref[:, span].astype(WIDE) + dot(q_ref[:, span], state) * mask
    mixed = whole_ref[...]
    mixed_ref[...] = mixed.astype(LOW)
    gated = (mixed * norm_factor(mixed) * u_ref[...].astype(WIDE)).astype(LOW)
    gated_ref[...] = gated.T

    @pl.when(step == 0)
    def _():
        finished(copies)

    x1 = x_ref[...].astype(WIDE) + dot(gated, w_ref[...])
    x1_ref[...] = x1.astype(LOW)
    h2 = (x1 * norm_factor(x1)).astype(LOW)
    h2_ref[...] = h2
    h2_turned_ref[...] = h2.T


def pair_kernel(tile, count, order_ref, h_ref, *refs):
    groups, refs = (refs[:count], refs[count : 2 * count]), refs[2 * count :]
    first_ref, second_ref, turned_ref, w_ref, sems = refs
    step, width = pl.program_id(0), first_ref.shape[1]

    def copies(at, layer):
        columns = pl.ds(pl.multiple_of(at * width, 128), width)
        return piece_copies(
            order_ref, groups[layer], 0, columns, w_ref.at[at, layer], sems.at[at, layer]
        )

    @pl.when(step == 0)
    def _():
        for at in range(w_ref.shape[0]):
            for layer in range(2):
                started(copies(at, layer))

    finished(copies(step, 0))
    first = dot(h_ref[...], w_ref[step, 0])
    first_ref[...] = first.astype(LOW)
    finished(copies(step, 1))
    for begin in range(0, h_ref.shape[0], tile):
        at = slice(begin, begin + tile)
        second = dot(h_ref[at, :], w_ref[step, 1])
        second_ref[at, :] = second.astype(LOW)
        turned_ref[:, at] = (first_ref[at, :].astype(WIDE) * second).astype(LOW).T


def pair(h, first_pieces, second_pieces, order, tile):
    (count, features), hidden = h.shape, first_pieces[0].shape[-1]
    steps = 2 if hidden % 256 == 0 else 1
    width, many = hidden // steps, len(first_pieces)
    block = pl.BlockSpec((count, width), lambda i, *_: (0, i))
    return call(
        functools.partial(pair_kernel, tile, many),
        [order],
        (steps,),
        [h, *first_pieces, *second_pieces],
        [pl.BlockSpec((count, features), lambda i, *_: (0, 0)), *[ANY] * (2 * many)],
        [shaped(count, hidden), shaped(count, hidden), shaped(hidden, count)],
        [block, block, pl.BlockSpec((width, count), lambda i, *_: (i, 0))],
        [
            pltpu.VMEM((steps, 2, features, width), LOW),
            pltpu.SemaphoreType.DMA((steps, 2, many)),
        ],
        4 * count * features * hidden,
    )


def down_back_kernel(count, order_ref, first_ref, second_ref, dy_ref, *refs):
    pieces, (dpair_ref, w_ref, sems) = refs[:count], refs[count:]
    copies = piece_copies(order_ref, pieces, 0, pl.ds(0, w_ref.shape[1]), w_ref, sems)

    @pl.when(pl.program_id(0) == 0)
    def _():
        started(copies)
        finished(copies)

    grad = dot(dy_ref[...], w_ref[...], 1, 1)
    dpair_ref[0] = (grad * second_ref[...].astype(WIDE)).astype(LOW)
    dpair_ref[1] = (grad * first_ref[...].astype(WIDE)).astype(LOW)


def down_back(first, second, dy, pieces, order, tile):
    (count, hidden), features = first.shape, dy.shape[1]
    wide, narrow = rows_spec(tile, hidden), rows_spec(tile, features)
    return call(
        functools.partial(down_back_kernel, len(pieces)),
        [order],
        (count // tile,),
        [first, second, dy, *pieces],
        [wide, wide, narrow, *[ANY] * len(pieces)],
        [shaped(2, count, hidden)],
        [pl.BlockSpec((2, tile, hidden), lambda i, *_: (0, i, 0))],
        [pltpu.VMEM((hidden, features), LOW), pltpu.SemaphoreType.DMA((len(pieces),))],
        2 * count * features * hidden,
    )[0]


def down_kernel(count, order_ref, first_ref, second_ref, x1_ref, *refs):
    pieces, (y_ref, w_ref, sems) = refs[:count], refs[count:]
    copies = piece_copies(order_ref, pieces, 0, pl.ds(0, w_ref.shape[1]), w_ref, sems)

    @pl.when(pl.program_id(0) == 0)
    def _():
        started(copies)
        finished(copies)

    glu = (first_ref[...].astype(WIDE) * second_ref[...].astype(WIDE)).astype(LOW)
    y_ref[...] = (x1_ref[...].astype(WIDE) + dot(glu, w_ref[...])).astype(LOW)


def down_forward(first, second, x1, pieces, order, tile):
    (count, hidden), features = first.shape, x1.shape[1]
    wide, narrow = rows_spec(tile, hidden), rows_spec(tile, features)
    return call(
        functools.partial(down_kernel, len(pieces)),
        [order],
        (count // tile,),
        [first, second, x1, *pieces],
        [wide, wide, narrow, *[ANY] * len(pieces)],
        [shaped(count, features)],
        [narrow],
        [pltpu.VMEM((hidden, features), LOW), pltpu.SemaphoreType.DMA((len(pieces),))],
        2 * count * features * hidden,
    )[0]


def pair_back_kernel(count, order_ref, dpair_ref, x1_ref, dy_ref, *refs):
    groups, (e1_ref, w_ref, sems) = (refs[:count], refs[count : 2 * count]), refs[2 * count :]
    step = pl.program_id(0)

    def copies(layer):
        return piece_copies(
            order_ref, groups[layer], 0, pl.ds(0, w_ref.shape[2]), w_ref.at[layer], sems.at[layer]
        )

    @pl.when(step == 0)
    def _():
        started(copies(0))
        started(copies(1))
        finished(copies(0))

    total = dot(dpair_ref[0], w_ref[0], 1, 1)

    @pl.when(step == 0)
    def _():
        finished(copies(1))

    total = total + dot(dpair_ref[1], w_ref[1], 1, 1)
    e1 = dy_ref[...].astype(WIDE) + norm_back(x1_ref[...].astype(WIDE), total)
    e1_ref[...] = e1.astype(LOW)


def pair_back(dpair, x1, dy, first_pieces, second_pieces, order, tile):
    (_, count, hidden), features, many = dpair.shape, x1.shape[1], len(first_pieces)
    narrow = rows_spec(tile, features)
    return call(
        functools.partial(pair_back_kernel, many),
        [order],
        (count // tile,),
        [dpair, x1, dy, *first_pieces, *second_pieces],
        [
            pl.BlockSpec((2, tile, hidden), lambda i, *_: (0, i, 0)),
            narrow,
            narrow,
            *[ANY] * (2 * many),
        ],
        [shaped(count, features)],
        [narrow],
        [pltpu.VMEM((2, features, hidden), LOW), pltpu.SemaphoreType.DMA((2, many))],
        4 * count * features * hidden,
    )[0]


def back_gate_kernel(
    docs,
    heads,
    count,
    start_ref,
    into_ref,
    out_ref,
    lengths_ref,
    order_ref,
    e1_ref,
    q_ref,
    u_ref,
    mixed_ref,
    *refs,
):
    pieces, (dmixed_ref, du_ref, grad_ref, w_ref, sems) = refs[:count], refs[count:]
    tokens, features = q_ref.shape
    head_dim = features // heads
    layer = pieces[0].shape[0] - 1
    copies = piece_copies(order_ref, pieces, layer, pl.ds(0, features), w_ref, sems)

    @pl.when(pl.program_id(0) == 0)
    def _():
        started(copies)
        finished(copies)

    dgated = dot(e1_ref[...], w_ref[...], 1, 1)
    mixed = mixed_ref[...].astype(WIDE)
    du_ref[...] = (dgated * (mixed * norm_factor(mixed))).astype(LOW)
    dmixed_ref[...] = norm_back(mixed, dgated * u_ref[...].astype(WIDE)).astype(LOW)
    _, entry_to = doc_bounds(lengths_ref, pl.program_id(0), docs, start_ref[0], tokens)
    mask = jnp.broadcast_to((column(tokens) < entry_to).astype(WIDE), (tokens, head_dim))
    for head in range(heads):
        span = slice(head * head_dim, (head + 1) * head_dim)
        queries = (q_ref[:, span].astype(WIDE) * mask).astype(LOW)
        grad_ref[0, head] = (dot(queries, dmixed_ref[:, span], 0, 0) * into_ref[head]).astype(LOW)


def back_mixing_kernel(
    docs,
    tile,
    heads,
    start_ref,
    into_ref,
    out_ref,
    lengths_ref,
    q_ref,
    slope_ref,
    k_ref,
    v_ref,
    dmixed_ref,
    state_ref,
    dq_ref,
    dk_ref,
    dv_ref,
    mask_ref,
    turned_ref,
):
    count, features = q_ref.shape
    head_dim = features // heads
    row, start = pl.program_id(0), start_ref[0]
    _, entry_to = doc_bounds(lengths_ref, row, docs, start, count)
    places = column(count)
    begin = doc_starts(lengths_ref, row, docs, start, places)
    across = lax.broadcasted_iota(jnp.int32, (count, count), 1)
    mask_ref[...] = ((across <= places) & (across >= begin)).astype(WIDE)
    flat = lax.broadcasted_iota(jnp.int32, (1, count), 1)
    begin = doc_starts(lengths_ref, row, docs, start, flat)
    down = lax.broadcasted_iota(jnp.int32, (count, count), 0)
    turned_ref[...] = ((down <= flat) & (down >= begin)).astype(WIDE)
    entry = jnp.broadcast_to((places < entry_to).astype(WIDE), (count, head_dim))
    for head in range(heads):
        span = slice(head * head_dim, (head + 1) * head_dim)
        state = (state_ref[0, head].astype(WIDE) * into_ref[head]).astype(LOW)
        for first in range(0, count, tile):
            upto = first + tile
            here = slice(first, upto)
            grads = dot(dmixed_ref[here, span], v_ref[:upto, span], 1, 1)
            dq = dot((grads * mask_ref[here, :upto]).astype(LOW), k_ref[:upto, span])
            dq = dq + dot(dmixed_ref[here, span], state, 1, 1) * entry[here]
            dq_ref[here, span] = (dq * slope_ref[here, span].astype(WIDE)).astype(LOW)
            turned = turned_ref[here, first:]
            grads = dot(v_ref[here, span], dmixed_ref[first:, span], 1, 1) * turned
            dk_ref[here, span] = dot(grads.astype(LOW), q_ref[first:, span]).astype(LOW)
            scores = dot(k_ref[here, span], q_ref[first:, span], 1, 1) * turned
            dv_ref[here, span] = dot(scores.astype(LOW), dmixed_ref[first:, span]).astype(LOW)


def back_finish_kernel(
    docs,
    heads,
    start_ref,
    into_ref,
    out_ref,
    lengths_ref,
    k_ref,
    slope_ref,
    v_ref,
    dk_part_ref,
    dv_part_ref,
    grad_ref,
    dk_ref,
    dv_ref,
):
    count, features = k_ref.shape
    head_dim = features // heads
    last_from, _ = doc_bounds(lengths_ref, pl.program_id(0), docs, start_ref[0], count)
    mask = jnp.broadcast_to((column(count) >= last_from).astype(WIDE), (count, head_dim))
    for head in range(heads):
        span = slice(head * head_dim, (head + 1) * head_dim)
        grad = (grad_ref[0, head].astype(WIDE) * out_ref[head]).astype(LOW)
        dk = dot(v_ref[:, span], grad, 1, 1) * mask + dk_part_ref[:, span].astype(WIDE)
        dk_ref[:, span] = (dk * slope_ref[:, span].astype(WIDE)).astype(LOW)
        dv = dot(k_ref[:, span], grad) * mask + dv_part_ref[:, span].astype(WIDE)
        dv_ref[:, span] = dv.astype(LOW)


def mixer_back_kernel(counts, order_ref, dq_ref, dk_ref, dv_ref, du_ref, x_ref, e1_ref, *refs):
    total = sum(counts)
    pieces, (out_ref, w_ref, sems) = refs[:total], refs[total:]
    groups = (pieces[: counts[0]], pieces[counts[0] :])
    grads = ((dk_ref, 0, 0), (dv_ref, 0, 1), (dq_ref, 1, 0), (du_ref, 1, 1))
    step, features = pl.program_id(0), x_ref.shape[1]

    def copies(index):
        _, group, layer = grads[index]
        return piece_copies(
            order_ref, groups[group], layer, pl.ds(0, features), w_ref.at[index], sems.at[index]
        )

    @pl.when(step == 0)
    def _():
        for index in range(4):
            started(copies(index))

    total = None
    for index in range(4):

        @pl.when(step == 0)
        def _(index=index):
            finished(copies(index))

        term = dot(grads[index][0][...], w_ref[index], 1, 1)
        total = term if total is None else total + term
    out_ref[...] = e1_ref[...].astype(WIDE) + norm_back(x_ref[...].astype(WIDE), total)


def mixer_back(grads, x, e1, key_value, rest, order, tile):
    count, features = x.shape
    spec = rows_spec(tile, features)
    pieces = [*key_value, *rest]
    return call(
        functools.partial(mixer_back_kernel, (len(key_value), len(rest))),
        [order],
        (count // tile,),
        [*grads, x, e1, *pieces],
        [spec] * 6 + [ANY] * len(pieces),
        [shaped(count, features, kind=WIDE)],
        [spec],
        [
            pltpu.VMEM((4, features, features), LOW),
            pltpu.SemaphoreType.DMA((4, len(key_value))),
        ],
        8 * count * features * features,
    )[0]


def block_grads_kernel(layers, mode, order_ref, turned_ref, *refs):
    members = len(layers)
    rights, refs = refs[:members], refs[members:]
    if mode == "keep":
        add_ref, *refs = refs
    *out_refs, left_ref, right_ref, left_sems, sems = refs
    member, half, at = pl.program_id(0), pl.program_id(1), pl.program_id(2)
    halves, whole = left_ref.shape[:2]
    width, tile, steps = whole // 4, right_ref.shape[-1], right_ref.shape[1]

    def left_copy(part, index):
        block = order_ref[part * 4 + index] * width
        return pltpu.make_async_copy(
            turned_ref.at[pl.ds(pl.multiple_of(block, width), width), :],
            left_ref.at[part, pl.ds(index * width, width), :],
            left_sems.at[part, index],
        )

    def right_copy(index, step):
        right = rights[index] if layers[index] is None else rights[index].at[layers[index]]
        return pltpu.make_async_copy(
            right.at[:, pl.ds(pl.multiple_of(step * tile, 128), tile)],
            right_ref.at[index, step],
            sems.at[index, step],
        )

    @pl.when((member == 0) & (half == 0) & (at == 0))
    def _():
        for index in range(4):
            left_copy(0, index).start()
        for index in range(members):
            for step in range(steps):
                right_copy(index, step).start()
        if halves == 2:
            for index in range(4):
                left_copy(1, index).start()
        for index in range(4):
            left_copy(0, index).wait()

    if halves == 2:

        @pl.when((member == 0) & (half == 1) & (at == 0))
        def _():
            for index in range(4):
                left_copy(1, index).wait()

    for index in range(members):

        @pl.when((member == index) & (half == 0))
        def _(index=index):
            right_copy(index, at).wait()

    term = dot(left_ref[half], right_ref[member, at])
    if mode == "keep":
        term = term + add_ref[0].astype(WIDE)
    term = term.astype(LOW)

    def keep(refs):
        for index, ref in enumerate(refs):
            ref[0] = term[index * width : (index + 1) * width]

    if mode == "send":
        out_refs[0][0] = term
    elif mode == "keep":
        keep(out_refs)
    else:

        @pl.when(half == 0)
        def _():
            out_refs[0][0] = term

        @pl.when(half == 1)
        def _():
            keep(out_refs[1:])


def block_grads(turned, rights, order, mode, received=None):
    (features, count), columns = turned.shape, rights[0][0].shape[-1]
    width, members = features // 8, len(rights)
    halves = 2 if mode == "both" else 1
    order = {"send": order[4:], "keep": order[:4], "both": jnp.roll(order, -4)}[mode]
    steps = 2 if columns % 256 == 0 and (columns > 1024 or members == 1) else 1
    tile, whole = columns // steps, features // 2

    def sent(i, part, j, *_):
        return i, 0, jnp.where(part == 0, j, steps - 1)

    def kept(i, part, j, *_):
        return i, 0, jnp.where(part == halves - 1, j, 0)

    send = shaped(members, whole, columns), pl.BlockSpec((1, whole, tile), sent)
    keep = shaped(members, width, columns), pl.BlockSpec((1, width, tile), kept)
    results = {"send": [send], "keep": [keep] * 4, "both": [send] + [keep] * 4}[mode]
    extra = [received] if mode == "keep" else []
    return call(
        functools.partial(block_grads_kernel, [layer for _, layer in rights], mode),
        [order],
        (members, halves, steps),
        [turned, *(right for right, _ in rights), *extra],
        [ANY] * (1 + members) + [send[1]] * len(extra),
        [shape for shape, _ in results],
        [spec for _, spec in results],
        [
            pltpu.VMEM((halves, whole, count), LOW),
            pltpu.VMEM((members, steps, count, tile), LOW),
            pltpu.SemaphoreType.DMA((halves, 4)),
            pltpu.SemaphoreType.DMA((members, steps)),
        ],
        2 * members * halves * count * whole * columns,
    )


def passed_along(value, steps):
    count = lax.axis_size("seq")
    leading, last = max(0, -steps), min(count, count - steps)
    return lax.ppermute(value, "seq", [(source, source + steps) for source in range(leading, last)])


def hops_needed(tokens):
    return min((LONGEST_DOC - 2) // tokens + 1, lax.axis_size("seq") - 1)


def side_steps(device):
    return (2, 4) if device % 2 == 0 else (4, 2)


def moved(value, kind):
    count = lax.axis_size("dp")
    if kind == "core":
        pairs = [(device, device ^ 1) for device in range(count)]
    else:
        pairs = [(device, device ^ side_steps(device)[kind]) for device in range(count)]
    return lax.ppermute(value, "dp", pairs)


def block_order():
    device = lax.axis_index("dp")
    table = []
    for index in range(8):
        row = []
        for mine in (index, index ^ 1):
            first, second = side_steps(mine)
            row += [mine, mine ^ first, mine ^ second, mine ^ first ^ second]
        table.append(row)
    return jnp.asarray(table, jnp.int32)[device]


def across_seq(value):
    count, place = lax.axis_size("seq"), lax.axis_index("seq")
    rows = value.shape[-2]
    if rows % count:
        return lax.psum(value, "seq")
    parts = value.reshape(*value.shape[:-2], count, rows // count, value.shape[-1])
    axis = parts.ndim - 3

    def shifted(part, step):
        return lax.ppermute(part, "seq", [(i, (i + step) % count) for i in range(count)])

    def taken(step):
        return lax.dynamic_index_in_dim(parts, (place + step) % count, axis, keepdims=False)

    total = plus(taken(0), *(shifted(taken(step), step) for step in range(1, count)))
    result = lax.dynamic_update_index_in_dim(parts, total, place, axis)
    for step in range(1, count):
        result = lax.dynamic_update_index_in_dim(
            result, shifted(total, step), (place - step) % count, axis
        )
    return result.reshape(value.shape)


def plus(*terms):
    return sum(term.astype(WIDE) for term in terms).astype(LOW)


class Scatter:
    def __init__(self, kept, received=None):
        self.kept, self.received = kept, received

    def block(self, index):
        if self.received is None:
            return [self.kept[index]]
        width = self.kept[index].shape[1]
        return [self.kept[index], self.received[:, index * width : (index + 1) * width]]

    def begin(self, *others):
        across, first = after(plus(*self.block(3)), *others), plus(*self.block(1))
        self.begun = across, first
        self.from_across, self.from_first = moved(across, 0), moved(first, 0)
        return self.begun

    def forward(self, *others):
        second = plus(*self.block(2), after(self.from_across, *others))
        self.from_second = moved(second, 1)
        return second

    def finish(self, *others):
        return plus(*self.block(0), self.from_first, after(self.from_second, *others))


def scattered_plainly(left, rights):
    terms = [
        lax.dot_general(left, right, (((1,), (0,)), ((), ())), preferred_element_type=WIDE)
        for right in rights
    ]
    return lax.psum_scatter(jnp.stack(terms).astype(LOW), "dp", scatter_dimension=1, tiled=True)


def local(
    hidden_in,
    mixer_weights,
    channel_in_weights,
    channel_out_weights,
    decay_rates,
    doc_lengths,
    out_cotangent,
):
    rows, tokens, features = hidden_in.shape
    heads = decay_rates.shape[1]
    head_dim = features // heads
    docs = doc_lengths.shape[1]
    count = rows * tokens
    tile = min(256, tokens)
    by_hand = lax.axis_size("dp") == 8
    order = block_order() if by_hand else jnp.zeros((1,), jnp.int32)
    rates = decay_rates[0]
    start = lax.axis_index("seq") * jnp.asarray(tokens, jnp.int32)
    centre = tokens // 2
    into = jnp.exp(-rates * (centre + 1))
    out = jnp.exp(-rates * (tokens - 1 - centre))
    scalars = [start[None], into, out, doc_lengths]
    ends = jnp.cumsum(doc_lengths, axis=1, dtype=jnp.int32)
    doc_before = jnp.sum((ends <= start - 1).astype(jnp.int32), axis=1)
    doc_last = jnp.sum((ends <= start + tokens - 1).astype(jnp.int32), axis=1)
    passing = jnp.where(
        (doc_before == doc_last)[:, None], jnp.exp(-rates * tokens)[None, :], 0.0
    )
    centred = (jnp.arange(tokens, dtype=jnp.int32) - centre).astype(WIDE)[:, None]
    spread = jnp.repeat(rates, head_dim)[None, :] * centred
    query_table, key_table = jnp.exp(-spread), jnp.exp(spread)

    big = min(512, count)

    def hop(message, steps):
        received = passed_along(message, steps).astype(WIDE)
        return received, (passing[..., None, None] * received).astype(LOW)

    def gather(piece, *others):
        if not by_hand:
            return [lax.all_gather(piece, "dp", axis=1, tiled=True)]
        piece = after(piece, *others) if others else piece
        return [piece, moved(piece, 0), moved(piece, 1)]

    def forward(pieces, *others):
        if not by_hand:
            return pieces
        mine = [*pieces, moved(after(pieces[1], *others) if others else pieces[1], 1)]
        return mine + [moved(part, "core") for part in mine]

    def arrived(pieces):
        return pieces[1:4]

    mixer = mixer_weights[0]
    key_value = forward(gather(mixer[1:3].astype(LOW)))
    rest = jnp.stack([mixer[0], mixer[3], mixer[4]]).astype(LOW)
    rest = gather(rest, *arrived(key_value))

    x = hidden_in.reshape(count, features)
    wide_x = x.astype(WIDE)
    h = (wide_x * norm_factor(wide_x)).astype(LOW)
    h_turned = h.T
    dy = out_cotangent.reshape(count, features)
    narrow, turned_out = shaped(count, features), shaped(features, count)
    states = shaped(rows, heads, head_dim, head_dim)
    row_spec = rows_spec(tokens, features)
    state_spec = pl.BlockSpec((1, heads, head_dim, head_dim), lambda i, *_: (i, 0, 0, 0))
    square = pltpu.VMEM((tokens, tokens), WIDE)
    hops = hops_needed(tokens)

    k, k_slope, v = project(h, key_table, key_value, order, tokens, tile)
    local_state = call(
        functools.partial(state_kernel, docs),
        scalars,
        (rows,),
        [k, v],
        [row_spec] * 2,
        [states],
        [state_spec],
        [],
        2 * count * features * head_dim,
    )[0]
    rest = forward(rest, local_state)
    first_w = gather(channel_in_weights[0, :1].astype(LOW), *arrived(rest))
    state_in, message = hop(local_state, 1)
    q, q_slope, u = project(after(h, message), query_table, rest, order, tokens, tile)
    first_w = forward(first_w, q)
    second_w = gather(channel_in_weights[0, 1:].astype(LOW), *arrived(first_w))
    part = call(
        functools.partial(mixing_kernel, docs, tile, heads),
        scalars,
        (rows,),
        [after(q, *first_w[1:3]), k, v],
        [row_spec] * 3,
        [narrow],
        [row_spec],
        [square],
        4 * count * features * tokens,
    )[0]
    for _ in range(hops - 1):
        received, message = hop(message, 1)
        state_in = state_in + after(received, part)
    spec = rows_spec(tile, features)
    turned_spec = pl.BlockSpec((features, tile), lambda i, *_: (0, i))
    steps = tokens // tile
    mixed, gated_turned, x1, h2, h2_turned = call(
        functools.partial(finish_kernel, docs, tokens, heads, len(rest)),
        [*scalars, order],
        (count // tile,),
        [q, u, part, x, state_in.astype(LOW), *rest],
        [spec] * 4
        + [
            pl.BlockSpec(
                (1, heads, head_dim, head_dim), lambda i, *_: (i // steps, 0, 0, 0)
            )
        ]
        + [ANY] * len(rest),
        [narrow, turned_out, narrow, narrow, turned_out],
        [spec, turned_spec, spec, spec, turned_spec],
        [
            pltpu.VMEM((tile, features), WIDE),
            pltpu.VMEM((features, features), LOW),
            pltpu.SemaphoreType.DMA((len(rest),)),
        ],
        2 * count * features * (features + head_dim),
    )
    second_w = forward(second_w, h2)
    down = gather(channel_out_weights.astype(LOW), *arrived(second_w))
    first, second, turned = pair(h2, first_w, second_w, order, tile)
    down = forward(down, first)

    down_grads = channel_grads = outer_grads = inner_grads = None
    if by_hand:
        sent, *kept = block_grads(turned, [(dy, None)], order, "both")
        down_grads = Scatter(kept, moved(sent, "core"))
        first = after(first, sent)
    dpair = down_back(first, second, dy, down, order, big)
    if by_hand:
        rights = [(dpair, 0), (dpair, 1)]
        begun = down_grads.begin(dpair)
        [sent] = block_grads(after(h2_turned, *begun), rights, order, "send")
        received = moved(sent, "core")
        y = down_forward(after(first, sent), second, x1, down, order, big)
        channel_grads = Scatter(block_grads(after(h2_turned, y), rights, order, "keep", received))
        begun = down_grads.forward(*channel_grads.kept), *channel_grads.begin()
        e1 = pair_back(after(dpair, *begun), x1, dy, first_w, second_w, order, big)
        down_part = down_grads.finish(e1)
        down_total = lax.psum(down_part, "seq")
        e1 = after(e1, down_part)
    else:
        y = down_forward(first, second, x1, down, order, big)
        down_total = lax.psum(scattered_plainly(turned, [dy]), "seq")
        e1 = pair_back(dpair, x1, dy, first_w, second_w, order, big)
        channel_total = lax.psum(scattered_plainly(h2_turned, [dpair[0], dpair[1]]), "seq")
    dmixed, du, local_grad = call(
        functools.partial(back_gate_kernel, docs, heads, len(rest)),
        [*scalars, order],
        (rows,),
        [e1, q, u, mixed, *rest],
        [row_spec] * 4 + [ANY] * len(rest),
        [narrow, narrow, states],
        [row_spec, row_spec, state_spec],
        [pltpu.VMEM((features, features), LOW), pltpu.SemaphoreType.DMA((len(rest),))],
        2 * count * features * (features + head_dim),
    )
    pins = []
    if by_hand:
        second_sent = channel_grads.forward(local_grad)
        sent_o, *kept_o = block_grads(
            after(gated_turned, second_sent, local_grad), [(e1, None)], order, "both"
        )
        received_o = moved(sent_o, "core")
        pins = [sent_o]
    state_grad, message = hop(local_grad, -1)
    message = after(message, *pins)
    dq, dk_part, dv_part = call(
        functools.partial(back_mixing_kernel, docs, tile, heads),
        scalars,
        (rows,),
        [q, q_slope, k, v, after(dmixed, message), state_in.astype(LOW)],
        [row_spec] * 5 + [state_spec],
        [narrow] * 3,
        [row_spec] * 3,
        [square] * 2,
        12 * count * features * tokens,
    )
    pins = [dq]
    if by_hand:
        channel_part = channel_grads.finish(dq)
        channel_total = lax.psum(after(channel_part, down_total), "seq")
        sent_uq, *kept_uq = block_grads(
            after(h_turned, channel_part), [(du, None), (dq, None)], order, "both"
        )
        received_uq = moved(sent_uq, "core")
        pins = [sent_uq]
    for _ in range(hops - 1):
        received, message = hop(message, -1)
        state_grad = state_grad + after(received, *pins)
    dk, dv = call(
        functools.partial(back_finish_kernel, docs, heads),
        scalars,
        (rows,),
        [k, k_slope, v, dk_part, dv_part, state_grad.astype(LOW)],
        [row_spec] * 5 + [state_spec],
        [narrow] * 2,
        [row_spec] * 2,
        [],
        4 * count * features * head_dim,
    )
    if by_hand:
        outer_grads = Scatter(
            [jnp.concatenate([a, b]) for a, b in zip(kept_uq, kept_o)],
            jnp.concatenate([received_uq, received_o]),
        )
        begun = outer_grads.begin(dk)
        sent_kv, *kept_kv = block_grads(
            after(h_turned, *begun), [(dk, None), (dv, None)], order, "both"
        )
        inner_grads = Scatter(kept_kv, moved(sent_kv, "core"))
        begun = inner_grads.begin(sent_kv)
        dq = after(dq, *begun)
    upstream = mixer_back([dq, dk, dv, du], x, e1, key_value, rest, order, big)
    if by_hand:
        outer_total = across_seq(outer_grads.finish(outer_grads.forward(upstream)))
        inner_total = across_seq(inner_grads.finish(inner_grads.forward(upstream)))
        mixer_gradient = jnp.stack(
            [outer_total[1], inner_total[0], inner_total[1], outer_total[0], outer_total[2]]
        )
    else:
        mixer_gradient = jnp.concatenate(
            [scattered_plainly(h_turned, [dq, dk, dv, du]), scattered_plainly(gated_turned, [e1])]
        )
        mixer_gradient = lax.psum(mixer_gradient, "seq")
    by_row = (rows, tokens, features)
    return (
        y.reshape(by_row),
        upstream.reshape(by_row),
        mixer_gradient.astype(WIDE)[None],
        channel_total.astype(WIDE)[None],
        down_total.astype(WIDE),
    )


def solution(mesh):
    in_specs = (
        P("dp", "seq", None),
        P(None, None, "dp", None),
        P(None, None, "dp", None),
        P(None, "dp", None),
        P(),
        P("dp", None),
        P("dp", "seq", None),
    )
    out_specs = (
        P("dp", "seq", None),
        P("dp", "seq", None),
        P(None, None, "dp", None),
        P(None, None, "dp", None),
        P(None, "dp", None),
    )
    return jax.shard_map(local, mesh=mesh, in_specs=in_specs, out_specs=out_specs, check_vma=False)
```

```python
import functools
import math

import jax
import jax.numpy as jnp
from jax import lax
from jax.experimental import pallas as pl
from jax.experimental.pallas import tpu as pltpu
from jax.sharding import PartitionSpec as P

EPS = 1e-06
LONGEST_DOC = 1024
LOW = jnp.bfloat16
WIDE = jnp.float32
VMEM_BYTES = 60 * 1024 * 1024
WEIGH = 50
ANY = pl.BlockSpec(memory_space=pl.ANY)


def dot(left, right, left_dim=1, right_dim=0):
    return lax.dot_general(
        left, right, (((left_dim,), (right_dim,)), ((), ())), preferred_element_type=WIDE
    )


def shaped(*shape, kind=LOW):
    return jax.ShapeDtypeStruct(shape, kind)


def vmem_needed(arrays, specs, scratch, spare):
    total = spare
    for array, spec in zip(arrays, specs):
        if spec.block_shape is not None:
            total += 2 * math.prod(spec.block_shape) * array.dtype.itemsize
    for ref in scratch:
        if ref.memory_space == pltpu.VMEM:
            total += math.prod(ref.shape) * jnp.dtype(ref.dtype).itemsize
    return min(total, VMEM_BYTES)


def call(kernel, scalars, grid, inputs, in_specs, outputs, out_specs, scratch, flops, spare=8):
    size = sum(a.size * a.dtype.itemsize for a in (*inputs, *outputs))
    limit = vmem_needed((*inputs, *outputs), (*in_specs, *out_specs), scratch, spare << 20)
    return pl.pallas_call(
        kernel,
        out_shape=outputs,
        grid_spec=pltpu.PrefetchScalarGridSpec(
            num_scalar_prefetch=len(scalars),
            grid=grid,
            in_specs=in_specs,
            out_specs=out_specs,
            scratch_shapes=scratch,
        ),
        compiler_params=pltpu.CompilerParams(vmem_limit_bytes=limit),
        cost_estimate=pl.CostEstimate(
            flops=int(flops) * WEIGH, bytes_accessed=int(size) * WEIGH, transcendentals=0
        ),
    )(*scalars, *inputs)


def rows_spec(tile, width):
    return pl.BlockSpec((tile, width), lambda i, *_: (i, 0))


def after(value, *others):
    return lax.optimization_barrier((value, *others))[0]


def piece_copies(order_ref, pieces, layers, columns, into_ref, sems):
    copies = []
    for index, piece in enumerate(pieces):
        rows = piece.shape[1]
        at = pl.ds(pl.multiple_of(order_ref[index] * rows, rows), rows)
        copies.append(
            pltpu.make_async_copy(
                piece.at[layers, :, columns], into_ref.at[..., at, :], sems.at[index]
            )
        )
    return copies


def started(copies):
    for copy in copies:
        copy.start()


def finished(copies):
    for copy in copies:
        copy.wait()


def doc_bounds(lengths_ref, row, docs, start, count):
    last = start + count - 1
    end = jnp.int32(0)
    last_from = jnp.int32(0)
    entry_to = jnp.int32(0)
    found = jnp.int32(0)
    for index in range(docs):
        end = end + lengths_ref[row, index]
        last_from = jnp.where(end <= last, end, last_from)
        ends_later = end > start - 1
        entry_to = jnp.where(ends_later & (found == 0), end, entry_to)
        found = jnp.where(ends_later, 1, found)
    return last_from - start, entry_to - start


def doc_starts(lengths_ref, row, docs, start, places):
    end = jnp.int32(0)
    begin = jnp.full(places.shape, -start, jnp.int32)
    for index in range(docs):
        end = end + lengths_ref[row, index]
        begin = jnp.where(places >= end - start, end - start, begin)
    return begin


def column(count, first=0):
    return first + lax.broadcasted_iota(jnp.int32, (count, 1), 0)


def project_kernel(tokens, tile, count, order_ref, h_ref, table_ref, *refs):
    pieces, (left_ref, slope_ref, right_ref, w_ref, sems) = refs[:count], refs[count:]
    step, width = pl.program_id(0), left_ref.shape[1]

    def copies(at):
        columns = pl.ds(pl.multiple_of(at * width, width), width)
        return piece_copies(
            order_ref, pieces, pl.ds(0, 2), columns, w_ref.at[at], sems.at[at]
        )

    @pl.when(step == 0)
    def _():
        for at in range(w_ref.shape[0]):
            started(copies(at))

    finished(copies(step))
    for first in range(0, h_ref.shape[0], tile):
        at = slice(first, first + tile)
        h = h_ref[at, :]
        pre = dot(h, w_ref[step, 0])
        gate = jax.nn.sigmoid(pre)
        decay = table_ref[first % tokens : first % tokens + tile, :].astype(WIDE)
        left_ref[at, :] = (pre * gate * decay).astype(LOW)
        slope_ref[at, :] = (gate * (1.0 + pre * (1.0 - gate)) * decay).astype(LOW)
        right_ref[at, :] = dot(h, w_ref[step, 1]).astype(LOW)


def project(h, table, pieces, order, tokens, tile):
    count, features = h.shape
    width = min(512, features)
    steps = features // width
    out = shaped(count, features)
    block = pl.BlockSpec((count, width), lambda i, *_: (0, i))
    return call(
        functools.partial(project_kernel, tokens, tile, len(pieces)),
        [order],
        (steps,),
        [h, table, *pieces],
        [
            pl.BlockSpec((count, features), lambda i, *_: (0, 0)),
            pl.BlockSpec((tokens, width), lambda i, *_: (0, i)),
            *[ANY] * len(pieces),
        ],
        [out] * 3,
        [block] * 3,
        [
            pltpu.VMEM((steps, 2, features, width), LOW),
            pltpu.SemaphoreType.DMA((steps, len(pieces))),
        ],
        4 * count * features * features,
    )


def state_kernel(docs, start_ref, into_ref, out_ref, lengths_ref, k_ref, v_ref, state_ref):
    count, head_dim = k_ref.shape[0], state_ref.shape[-1]
    last_from, _ = doc_bounds(lengths_ref, pl.program_id(0), docs, start_ref[0], count)
    mask = jnp.broadcast_to((column(count) >= last_from).astype(WIDE), (count, head_dim))
    for head in range(state_ref.shape[1]):
        span = slice(head * head_dim, (head + 1) * head_dim)
        keys = (k_ref[:, span].astype(WIDE) * mask).astype(LOW)
        state_ref[0, head] = (dot(keys, v_ref[:, span], 0, 0) * out_ref[head]).astype(LOW)


def mixing_kernel(
    docs, tile, heads, start_ref, into_ref, out_ref, lengths_ref, q_ref, k_ref, v_ref, o_ref, mask_ref
):
    count, features = q_ref.shape
    head_dim = features // heads
    places = column(count)
    begin = doc_starts(lengths_ref, pl.program_id(0), docs, start_ref[0], places)
    across = lax.broadcasted_iota(jnp.int32, (count, count), 1)
    mask_ref[...] = ((across <= places) & (across >= begin)).astype(WIDE)
    for head in range(heads):
        span = slice(head * head_dim, (head + 1) * head_dim)
        for first in range(0, count, tile):
            upto = first + tile
            scores = dot(q_ref[first:upto, span], k_ref[:upto, span], 1, 1)
            scores = (scores * mask_ref[first:upto, :upto]).astype(LOW)
            o_ref[first:upto, span] = dot(scores, v_ref[:upto, span]).astype(LOW)


def norm_factor(value_rows):
    return lax.rsqrt(jnp.mean(value_rows * value_rows, axis=-1, keepdims=True) + EPS)


def norm_back(value_rows, upstream):
    factor = norm_factor(value_rows)
    inner = jnp.mean(upstream * value_rows, axis=-1, keepdims=True)
    return factor * upstream - (factor * factor * factor * inner) * value_rows


def finish_kernel(
    docs,
    tokens,
    heads,
    count,
    start_ref,
    into_ref,
    out_ref,
    lengths_ref,
    order_ref,
    q_ref,
    u_ref,
    part_ref,
    x_ref,
    state_ref,
    *refs,
):
    pieces = refs[:count]
    mixed_ref, gated_ref, x1_ref, h2_ref, h2_turned_ref, whole_ref, w_ref, sems = refs[count:]
    tile, features = q_ref.shape
    head_dim = features // heads
    step, steps = pl.program_id(0), tokens // tile
    layer = pieces[0].shape[0] - 1
    copies = piece_copies(order_ref, pieces, layer, pl.ds(0, features), w_ref, sems)

    @pl.when(step == 0)
    def _():
        started(copies)

    row = step // steps
    _, entry_to = doc_bounds(lengths_ref, row, docs, start_ref[0], tokens)
    mask = (column(tile, (step % steps) * tile) < entry_to).astype(WIDE)
    mask = jnp.broadcast_to(mask, (tile, head_dim))
    for head in range(heads):
        span = slice(head * head_dim, (head + 1) * head_dim)
        state = (state_ref[0, head].astype(WIDE) * into_ref[head]).astype(LOW)
        whole_ref[:, span] = part_ref[:, span].astype(WIDE) + dot(q_ref[:, span], state) * mask
    mixed = whole_ref[...]
    mixed_ref[...] = mixed.astype(LOW)
    gated = (mixed * norm_factor(mixed) * u_ref[...].astype(WIDE)).astype(LOW)
    gated_ref[...] = gated.T

    @pl.when(step == 0)
    def _():
        finished(copies)

    x1 = x_ref[...].astype(WIDE) + dot(gated, w_ref[...])
    x1_ref[...] = x1.astype(LOW)
    h2 = (x1 * norm_factor(x1)).astype(LOW)
    h2_ref[...] = h2
    h2_turned_ref[...] = h2.T


def pair_kernel(tile, count, order_ref, h_ref, *refs):
    groups, refs = (refs[:count], refs[count : 2 * count]), refs[2 * count :]
    first_ref, second_ref, turned_ref, w_ref, sems = refs
    step, width = pl.program_id(0), first_ref.shape[1]

    def copies(at, layer):
        columns = pl.ds(pl.multiple_of(at * width, 128), width)
        return piece_copies(
            order_ref, groups[layer], 0, columns, w_ref.at[at, layer], sems.at[at, layer]
        )

    @pl.when(step == 0)
    def _():
        for at in range(w_ref.shape[0]):
            for layer in range(2):
                started(copies(at, layer))

    finished(copies(step, 0))
    first = dot(h_ref[...], w_ref[step, 0])
    first_ref[...] = first.astype(LOW)
    finished(copies(step, 1))
    for begin in range(0, h_ref.shape[0], tile):
        at = slice(begin, begin + tile)
        second = dot(h_ref[at, :], w_ref[step, 1])
        second_ref[at, :] = second.astype(LOW)
        turned_ref[:, at] = (first_ref[at, :].astype(WIDE) * second).astype(LOW).T


def pair(h, first_pieces, second_pieces, order, tile):
    (count, features), hidden = h.shape, first_pieces[0].shape[-1]
    steps = 2 if hidden % 256 == 0 else 1
    width, many = hidden // steps, len(first_pieces)
    block = pl.BlockSpec((count, width), lambda i, *_: (0, i))
    return call(
        functools.partial(pair_kernel, tile, many),
        [order],
        (steps,),
        [h, *first_pieces, *second_pieces],
        [pl.BlockSpec((count, features), lambda i, *_: (0, 0)), *[ANY] * (2 * many)],
        [shaped(count, hidden), shaped(count, hidden), shaped(hidden, count)],
        [block, block, pl.BlockSpec((width, count), lambda i, *_: (i, 0))],
        [
            pltpu.VMEM((steps, 2, features, width), LOW),
            pltpu.SemaphoreType.DMA((steps, 2, many)),
        ],
        4 * count * features * hidden,
    )


def down_back_kernel(count, order_ref, first_ref, second_ref, dy_ref, *refs):
    pieces, (dpair_ref, w_ref, sems) = refs[:count], refs[count:]
    copies = piece_copies(order_ref, pieces, 0, pl.ds(0, w_ref.shape[1]), w_ref, sems)

    @pl.when(pl.program_id(0) == 0)
    def _():
        started(copies)
        finished(copies)

    grad = dot(dy_ref[...], w_ref[...], 1, 1)
    dpair_ref[0] = (grad * second_ref[...].astype(WIDE)).astype(LOW)
    dpair_ref[1] = (grad * first_ref[...].astype(WIDE)).astype(LOW)


def down_back(first, second, dy, pieces, order, tile):
    (count, hidden), features = first.shape, dy.shape[1]
    wide, narrow = rows_spec(tile, hidden), rows_spec(tile, features)
    return call(
        functools.partial(down_back_kernel, len(pieces)),
        [order],
        (count // tile,),
        [first, second, dy, *pieces],
        [wide, wide, narrow, *[ANY] * len(pieces)],
        [shaped(2, count, hidden)],
        [pl.BlockSpec((2, tile, hidden), lambda i, *_: (0, i, 0))],
        [pltpu.VMEM((hidden, features), LOW), pltpu.SemaphoreType.DMA((len(pieces),))],
        2 * count * features * hidden,
    )[0]


def down_kernel(count, order_ref, first_ref, second_ref, x1_ref, *refs):
    pieces, (y_ref, w_ref, sems) = refs[:count], refs[count:]
    copies = piece_copies(order_ref, pieces, 0, pl.ds(0, w_ref.shape[1]), w_ref, sems)

    @pl.when(pl.program_id(0) == 0)
    def _():
        started(copies)
        finished(copies)

    glu = (first_ref[...].astype(WIDE) * second_ref[...].astype(WIDE)).astype(LOW)
    y_ref[...] = (x1_ref[...].astype(WIDE) + dot(glu, w_ref[...])).astype(LOW)


def down_forward(first, second, x1, pieces, order, tile):
    (count, hidden), features = first.shape, x1.shape[1]
    wide, narrow = rows_spec(tile, hidden), rows_spec(tile, features)
    return call(
        functools.partial(down_kernel, len(pieces)),
        [order],
        (count // tile,),
        [first, second, x1, *pieces],
        [wide, wide, narrow, *[ANY] * len(pieces)],
        [shaped(count, features)],
        [narrow],
        [pltpu.VMEM((hidden, features), LOW), pltpu.SemaphoreType.DMA((len(pieces),))],
        2 * count * features * hidden,
    )[0]


def pair_back_kernel(count, order_ref, dpair_ref, x1_ref, dy_ref, *refs):
    groups, (e1_ref, w_ref, sems) = (refs[:count], refs[count : 2 * count]), refs[2 * count :]
    step = pl.program_id(0)

    def copies(layer):
        return piece_copies(
            order_ref, groups[layer], 0, pl.ds(0, w_ref.shape[2]), w_ref.at[layer], sems.at[layer]
        )

    @pl.when(step == 0)
    def _():
        started(copies(0))
        started(copies(1))
        finished(copies(0))

    total = dot(dpair_ref[0], w_ref[0], 1, 1)

    @pl.when(step == 0)
    def _():
        finished(copies(1))

    total = total + dot(dpair_ref[1], w_ref[1], 1, 1)
    e1 = dy_ref[...].astype(WIDE) + norm_back(x1_ref[...].astype(WIDE), total)
    e1_ref[...] = e1.astype(LOW)


def pair_back(dpair, x1, dy, first_pieces, second_pieces, order, tile):
    (_, count, hidden), features, many = dpair.shape, x1.shape[1], len(first_pieces)
    narrow = rows_spec(tile, features)
    return call(
        functools.partial(pair_back_kernel, many),
        [order],
        (count // tile,),
        [dpair, x1, dy, *first_pieces, *second_pieces],
        [
            pl.BlockSpec((2, tile, hidden), lambda i, *_: (0, i, 0)),
            narrow,
            narrow,
            *[ANY] * (2 * many),
        ],
        [shaped(count, features)],
        [narrow],
        [pltpu.VMEM((2, features, hidden), LOW), pltpu.SemaphoreType.DMA((2, many))],
        4 * count * features * hidden,
    )[0]


def back_gate_kernel(
    docs,
    heads,
    count,
    start_ref,
    into_ref,
    out_ref,
    lengths_ref,
    order_ref,
    e1_ref,
    q_ref,
    u_ref,
    mixed_ref,
    *refs,
):
    pieces, (dmixed_ref, du_ref, grad_ref, w_ref, sems) = refs[:count], refs[count:]
    tokens, features = q_ref.shape
    head_dim = features // heads
    layer = pieces[0].shape[0] - 1
    copies = piece_copies(order_ref, pieces, layer, pl.ds(0, features), w_ref, sems)

    @pl.when(pl.program_id(0) == 0)
    def _():
        started(copies)
        finished(copies)

    dgated = dot(e1_ref[...], w_ref[...], 1, 1)
    mixed = mixed_ref[...].astype(WIDE)
    du_ref[...] = (dgated * (mixed * norm_factor(mixed))).astype(LOW)
    dmixed_ref[...] = norm_back(mixed, dgated * u_ref[...].astype(WIDE)).astype(LOW)
    _, entry_to = doc_bounds(lengths_ref, pl.program_id(0), docs, start_ref[0], tokens)
    mask = jnp.broadcast_to((column(tokens) < entry_to).astype(WIDE), (tokens, head_dim))
    for head in range(heads):
        span = slice(head * head_dim, (head + 1) * head_dim)
        queries = (q_ref[:, span].astype(WIDE) * mask).astype(LOW)
        grad_ref[0, head] = (dot(queries, dmixed_ref[:, span], 0, 0) * into_ref[head]).astype(LOW)


def back_mixing_kernel(
    docs,
    tile,
    heads,
    start_ref,
    into_ref,
    out_ref,
    lengths_ref,
    q_ref,
    slope_ref,
    k_ref,
    v_ref,
    dmixed_ref,
    state_ref,
    dq_ref,
    dk_ref,
    dv_ref,
    mask_ref,
    turned_ref,
):
    count, features = q_ref.shape
    head_dim = features // heads
    row, start = pl.program_id(0), start_ref[0]
    _, entry_to = doc_bounds(lengths_ref, row, docs, start, count)
    places = column(count)
    begin = doc_starts(lengths_ref, row, docs, start, places)
    across = lax.broadcasted_iota(jnp.int32, (count, count), 1)
    mask_ref[...] = ((across <= places) & (across >= begin)).astype(WIDE)
    flat = lax.broadcasted_iota(jnp.int32, (1, count), 1)
    begin = doc_starts(lengths_ref, row, docs, start, flat)
    down = lax.broadcasted_iota(jnp.int32, (count, count), 0)
    turned_ref[...] = ((down <= flat) & (down >= begin)).astype(WIDE)
    entry = jnp.broadcast_to((places < entry_to).astype(WIDE), (count, head_dim))
    for head in range(heads):
        span = slice(head * head_dim, (head + 1) * head_dim)
        state = (state_ref[0, head].astype(WIDE) * into_ref[head]).astype(LOW)
        for first in range(0, count, tile):
            upto = first + tile
            here = slice(first, upto)
            grads = dot(dmixed_ref[here, span], v_ref[:upto, span], 1, 1)
            dq = dot((grads * mask_ref[here, :upto]).astype(LOW), k_ref[:upto, span])
            dq = dq + dot(dmixed_ref[here, span], state, 1, 1) * entry[here]
            dq_ref[here, span] = (dq * slope_ref[here, span].astype(WIDE)).astype(LOW)
            turned = turned_ref[here, first:]
            grads = dot(v_ref[here, span], dmixed_ref[first:, span], 1, 1) * turned
            dk_ref[here, span] = dot(grads.astype(LOW), q_ref[first:, span]).astype(LOW)
            scores = dot(k_ref[here, span], q_ref[first:, span], 1, 1) * turned
            dv_ref[here, span] = dot(scores.astype(LOW), dmixed_ref[first:, span]).astype(LOW)


def back_finish_kernel(
    docs,
    heads,
    start_ref,
    into_ref,
    out_ref,
    lengths_ref,
    k_ref,
    slope_ref,
    v_ref,
    dk_part_ref,
    dv_part_ref,
    grad_ref,
    dk_ref,
    dv_ref,
):
    count, features = k_ref.shape
    head_dim = features // heads
    last_from, _ = doc_bounds(lengths_ref, pl.program_id(0), docs, start_ref[0], count)
    mask = jnp.broadcast_to((column(count) >= last_from).astype(WIDE), (count, head_dim))
    for head in range(heads):
        span = slice(head * head_dim, (head + 1) * head_dim)
        grad = (grad_ref[0, head].astype(WIDE) * out_ref[head]).astype(LOW)
        dk = dot(v_ref[:, span], grad, 1, 1) * mask + dk_part_ref[:, span].astype(WIDE)
        dk_ref[:, span] = (dk * slope_ref[:, span].astype(WIDE)).astype(LOW)
        dv = dot(k_ref[:, span], grad) * mask + dv_part_ref[:, span].astype(WIDE)
        dv_ref[:, span] = dv.astype(LOW)


def mixer_back_kernel(counts, order_ref, dq_ref, dk_ref, dv_ref, du_ref, x_ref, e1_ref, *refs):
    total = sum(counts)
    pieces, (out_ref, w_ref, sems) = refs[:total], refs[total:]
    groups = (pieces[: counts[0]], pieces[counts[0] :])
    grads = ((dk_ref, 0, 0), (dv_ref, 0, 1), (dq_ref, 1, 0), (du_ref, 1, 1))
    step, features = pl.program_id(0), x_ref.shape[1]

    def copies(index):
        _, group, layer = grads[index]
        return piece_copies(
            order_ref, groups[group], layer, pl.ds(0, features), w_ref.at[index], sems.at[index]
        )

    @pl.when(step == 0)
    def _():
        for index in range(4):
            started(copies(index))

    total = None
    for index in range(4):

        @pl.when(step == 0)
        def _(index=index):
            finished(copies(index))

        term = dot(grads[index][0][...], w_ref[index], 1, 1)
        total = term if total is None else total + term
    out_ref[...] = e1_ref[...].astype(WIDE) + norm_back(x_ref[...].astype(WIDE), total)


def mixer_back(grads, x, e1, key_value, rest, order, tile):
    count, features = x.shape
    spec = rows_spec(tile, features)
    pieces = [*key_value, *rest]
    return call(
        functools.partial(mixer_back_kernel, (len(key_value), len(rest))),
        [order],
        (count // tile,),
        [*grads, x, e1, *pieces],
        [spec] * 6 + [ANY] * len(pieces),
        [shaped(count, features, kind=WIDE)],
        [spec],
        [
            pltpu.VMEM((4, features, features), LOW),
            pltpu.SemaphoreType.DMA((4, len(key_value))),
        ],
        8 * count * features * features,
    )[0]


def block_grads_kernel(layers, mode, order_ref, turned_ref, *refs):
    members = len(layers)
    rights, refs = refs[:members], refs[members:]
    if mode == "keep":
        add_ref, *refs = refs
    *out_refs, left_ref, right_ref, left_sems, sems = refs
    member, half, at = pl.program_id(0), pl.program_id(1), pl.program_id(2)
    halves, whole = left_ref.shape[:2]
    width, tile, steps = whole // 4, right_ref.shape[-1], right_ref.shape[1]

    def left_copy(part, index):
        block = order_ref[part * 4 + index] * width
        return pltpu.make_async_copy(
            turned_ref.at[pl.ds(pl.multiple_of(block, width), width), :],
            left_ref.at[part, pl.ds(index * width, width), :],
            left_sems.at[part, index],
        )

    def right_copy(index, step):
        right = rights[index] if layers[index] is None else rights[index].at[layers[index]]
        return pltpu.make_async_copy(
            right.at[:, pl.ds(pl.multiple_of(step * tile, 128), tile)],
            right_ref.at[index, step],
            sems.at[index, step],
        )

    @pl.when((member == 0) & (half == 0) & (at == 0))
    def _():
        for index in range(4):
            left_copy(0, index).start()
        for index in range(members):
            for step in range(steps):
                right_copy(index, step).start()
        if halves == 2:
            for index in range(4):
                left_copy(1, index).start()
        for index in range(4):
            left_copy(0, index).wait()

    if halves == 2:

        @pl.when((member == 0) & (half == 1) & (at == 0))
        def _():
            for index in range(4):
                left_copy(1, index).wait()

    for index in range(members):

        @pl.when((member == index) & (half == 0))
        def _(index=index):
            right_copy(index, at).wait()

    term = dot(left_ref[half], right_ref[member, at])
    if mode == "keep":
        term = term + add_ref[0].astype(WIDE)
    term = term.astype(LOW)

    def keep(refs):
        for index, ref in enumerate(refs):
            ref[0] = term[index * width : (index + 1) * width]

    if mode == "send":
        out_refs[0][0] = term
    elif mode == "keep":
        keep(out_refs)
    else:

        @pl.when(half == 0)
        def _():
            out_refs[0][0] = term

        @pl.when(half == 1)
        def _():
            keep(out_refs[1:])


def block_grads(turned, rights, order, mode, received=None):
    (features, count), columns = turned.shape, rights[0][0].shape[-1]
    width, members = features // 8, len(rights)
    halves = 2 if mode == "both" else 1
    order = {"send": order[4:], "keep": order[:4], "both": jnp.roll(order, -4)}[mode]
    steps = 2 if columns % 256 == 0 and (columns > 1024 or members == 1) else 1
    tile, whole = columns // steps, features // 2

    def sent(i, part, j, *_):
        return i, 0, jnp.where(part == 0, j, steps - 1)

    def kept(i, part, j, *_):
        return i, 0, jnp.where(part == halves - 1, j, 0)

    send = shaped(members, whole, columns), pl.BlockSpec((1, whole, tile), sent)
    keep = shaped(members, width, columns), pl.BlockSpec((1, width, tile), kept)
    results = {"send": [send], "keep": [keep] * 4, "both": [send] + [keep] * 4}[mode]
    extra = [received] if mode == "keep" else []
    return call(
        functools.partial(block_grads_kernel, [layer for _, layer in rights], mode),
        [order],
        (members, halves, steps),
        [turned, *(right for right, _ in rights), *extra],
        [ANY] * (1 + members) + [send[1]] * len(extra),
        [shape for shape, _ in results],
        [spec for _, spec in results],
        [
            pltpu.VMEM((halves, whole, count), LOW),
            pltpu.VMEM((members, steps, count, tile), LOW),
            pltpu.SemaphoreType.DMA((halves, 4)),
            pltpu.SemaphoreType.DMA((members, steps)),
        ],
        2 * members * halves * count * whole * columns,
    )


def passed_along(value, steps):
    count = lax.axis_size("seq")
    leading, last = max(0, -steps), min(count, count - steps)
    return lax.ppermute(value, "seq", [(source, source + steps) for source in range(leading, last)])


def hops_needed(tokens):
    return min((LONGEST_DOC - 2) // tokens + 1, lax.axis_size("seq") - 1)


def side_steps(device):
    return (2, 4) if device % 2 == 0 else (4, 2)


def moved(value, kind):
    count = lax.axis_size("dp")
    if kind == "core":
        pairs = [(device, device ^ 1) for device in range(count)]
    else:
        pairs = [(device, device ^ side_steps(device)[kind]) for device in range(count)]
    return lax.ppermute(value, "dp", pairs)


def block_order():
    device = lax.axis_index("dp")
    table = []
    for index in range(8):
        row = []
        for mine in (index, index ^ 1):
            first, second = side_steps(mine)
            row += [mine, mine ^ first, mine ^ second, mine ^ first ^ second]
        table.append(row)
    return jnp.asarray(table, jnp.int32)[device]


class SeqSum:
    def __init__(self, value):
        members, rows, columns = value.shape
        self.count, self.place = lax.axis_size("seq"), lax.axis_index("seq")
        self.shape = value.shape
        self.parts = value.reshape(members, self.count, rows // self.count, columns)
        self.received = [
            self.shifted(self.taken(step), step) for step in range(1, self.count)
        ]

    def shifted(self, part, step):
        pairs = [(i, (i + step) % self.count) for i in range(self.count)]
        return lax.ppermute(part, "seq", pairs)

    def taken(self, step):
        index = (self.place + step) % self.count
        return lax.dynamic_index_in_dim(self.parts, index, 1, keepdims=False)

    def share(self, *others):
        total = plus(self.taken(0), *after(tuple(self.received), *others))
        self.totals = [total] + [self.shifted(total, step) for step in range(1, self.count)]
        return total

    def finish(self, *others):
        totals = [total.astype(WIDE) for total in after(tuple(self.totals), *others)]
        parts = [
            lax.select_n((self.place - index) % self.count, *totals)
            for index in range(self.count)
        ]
        return jnp.stack(parts, axis=1).reshape(self.shape)


def plus(*terms):
    return sum(term.astype(WIDE) for term in terms).astype(LOW)


class Scatter:
    def __init__(self, kept, received=None):
        self.kept, self.received = kept, received

    def block(self, index):
        if self.received is None:
            return [self.kept[index]]
        width = self.kept[index].shape[1]
        return [self.kept[index], self.received[:, index * width : (index + 1) * width]]

    def begin(self, *others):
        across, first = after(plus(*self.block(3)), *others), plus(*self.block(1))
        self.begun = across, first
        self.from_across, self.from_first = moved(across, 0), moved(first, 0)
        return self.begun

    def forward(self, *others):
        second = plus(*self.block(2), after(self.from_across, self.from_first, *others))
        self.from_second = moved(second, 1)
        return second

    def finish(self, *others):
        return plus(*self.block(0), self.from_first, after(self.from_second, *others))


def scattered_plainly(left, rights):
    terms = [
        lax.dot_general(left, right, (((1,), (0,)), ((), ())), preferred_element_type=WIDE)
        for right in rights
    ]
    return lax.psum_scatter(jnp.stack(terms).astype(LOW), "dp", scatter_dimension=1, tiled=True)


def local(
    hidden_in,
    mixer_weights,
    channel_in_weights,
    channel_out_weights,
    decay_rates,
    doc_lengths,
    out_cotangent,
):
    rows, tokens, features = hidden_in.shape
    heads = decay_rates.shape[1]
    head_dim = features // heads
    docs = doc_lengths.shape[1]
    count = rows * tokens
    tile = min(256, tokens)
    by_hand = lax.axis_size("dp") == 8
    order = block_order() if by_hand else jnp.zeros((1,), jnp.int32)
    rates = decay_rates[0]
    start = lax.axis_index("seq") * jnp.asarray(tokens, jnp.int32)
    centre = tokens // 2
    into = jnp.exp(-rates * (centre + 1))
    out = jnp.exp(-rates * (tokens - 1 - centre))
    scalars = [start[None], into, out, doc_lengths]
    ends = jnp.cumsum(doc_lengths, axis=1, dtype=jnp.int32)
    doc_before = jnp.sum((ends <= start - 1).astype(jnp.int32), axis=1)
    doc_last = jnp.sum((ends <= start + tokens - 1).astype(jnp.int32), axis=1)
    passing = jnp.where(
        (doc_before == doc_last)[:, None], jnp.exp(-rates * tokens)[None, :], 0.0
    )
    centred = (jnp.arange(tokens, dtype=jnp.int32) - centre).astype(WIDE)[:, None]
    spread = jnp.repeat(rates, head_dim)[None, :] * centred
    query_table, key_table = jnp.exp(-spread), jnp.exp(spread)

    big = min(512, count)

    def hop(message, steps, *others):
        received = after(passed_along(message, steps), *others).astype(WIDE)
        return received, (passing[..., None, None] * received).astype(LOW)

    def gather(piece, *others):
        if not by_hand:
            return [lax.all_gather(piece, "dp", axis=1, tiled=True)]
        piece = after(piece, *others) if others else piece
        return [piece, moved(piece, 0), moved(piece, 1)]

    def forward(pieces, *others):
        if not by_hand:
            return pieces
        mine = [*pieces, moved(after(pieces[1], *others) if others else pieces[1], 1)]
        return mine + [moved(part, "core") for part in mine]

    def arrived(pieces):
        return pieces[1:4]

    mixer = mixer_weights[0]
    key_value = forward(gather(mixer[1:3].astype(LOW)))
    rest = jnp.stack([mixer[0], mixer[3], mixer[4]]).astype(LOW)
    rest = gather(rest, *arrived(key_value))

    x = hidden_in.reshape(count, features)
    wide_x = x.astype(WIDE)
    h = (wide_x * norm_factor(wide_x)).astype(LOW)
    h_turned = h.T
    dy = out_cotangent.reshape(count, features)
    narrow, turned_out = shaped(count, features), shaped(features, count)
    states = shaped(rows, heads, head_dim, head_dim)
    row_spec = rows_spec(tokens, features)
    state_spec = pl.BlockSpec((1, heads, head_dim, head_dim), lambda i, *_: (i, 0, 0, 0))
    square = pltpu.VMEM((tokens, tokens), WIDE)
    hops = hops_needed(tokens)

    k, k_slope, v = project(h, key_table, key_value, order, tokens, tile)
    local_state = call(
        functools.partial(state_kernel, docs),
        scalars,
        (rows,),
        [k, v],
        [row_spec] * 2,
        [states],
        [state_spec],
        [],
        2 * count * features * head_dim,
    )[0]
    rest = forward(rest, local_state)
    first_w = gather(channel_in_weights[0, :1].astype(LOW), *arrived(rest))
    state_in, message = hop(local_state, 1)
    q, q_slope, u = project(after(h, message), query_table, rest, order, tokens, tile)
    first_w = forward(first_w, q)
    second_w = gather(channel_in_weights[0, 1:].astype(LOW), *arrived(first_w))
    part = call(
        functools.partial(mixing_kernel, docs, tile, heads),
        scalars,
        (rows,),
        [after(q, *first_w[1:3]), k, v],
        [row_spec] * 3,
        [narrow],
        [row_spec],
        [square],
        4 * count * features * tokens,
    )[0]
    for _ in range(hops - 1):
        received, message = hop(message, 1)
        state_in = state_in + after(received, part)
    spec = rows_spec(tile, features)
    turned_spec = pl.BlockSpec((features, tile), lambda i, *_: (0, i))
    steps = tokens // tile
    mixed, gated_turned, x1, h2, h2_turned = call(
        functools.partial(finish_kernel, docs, tokens, heads, len(rest)),
        [*scalars, order],
        (count // tile,),
        [q, u, part, x, state_in.astype(LOW), *rest],
        [spec] * 4
        + [
            pl.BlockSpec(
                (1, heads, head_dim, head_dim), lambda i, *_: (i // steps, 0, 0, 0)
            )
        ]
        + [ANY] * len(rest),
        [narrow, turned_out, narrow, narrow, turned_out],
        [spec, turned_spec, spec, spec, turned_spec],
        [
            pltpu.VMEM((tile, features), WIDE),
            pltpu.VMEM((features, features), LOW),
            pltpu.SemaphoreType.DMA((len(rest),)),
        ],
        2 * count * features * (features + head_dim),
    )
    second_w = forward(second_w, part)
    down = gather(channel_out_weights.astype(LOW), *arrived(second_w))
    first, second, turned = pair(h2, first_w, second_w, order, tile)
    down = forward(down, first)

    down_grads = channel_grads = outer_grads = inner_grads = None
    if by_hand:
        sent, *kept = block_grads(turned, [(after(dy, *down[1:3]), None)], order, "both")
        down_grads = Scatter(kept, moved(sent, "core"))
        first = after(first, sent)
    dpair = down_back(first, second, dy, down, order, big)
    if by_hand:
        rights = [(dpair, 0), (dpair, 1)]
        begun = down_grads.begin(dpair)
        [sent] = block_grads(after(h2_turned, *begun), rights, order, "send")
        received = moved(sent, "core")
        e1 = pair_back(after(dpair, sent), x1, dy, first_w, second_w, order, big)
        begun = down_grads.forward(e1)
        channel_grads = Scatter(
            block_grads(after(h2_turned, begun), rights, order, "keep", received)
        )
        begun = channel_grads.begin()
        down_part = down_grads.finish(*channel_grads.kept)
        down_sum = SeqSum(down_part)
        e1 = after(e1, down_part, *begun)
    else:
        y = down_forward(first, second, x1, down, order, big)
        down_total = lax.psum(scattered_plainly(turned, [dy]), "seq")
        e1 = pair_back(dpair, x1, dy, first_w, second_w, order, big)
        channel_total = lax.psum(scattered_plainly(h2_turned, [dpair[0], dpair[1]]), "seq")
    dmixed, du, local_grad = call(
        functools.partial(back_gate_kernel, docs, heads, len(rest)),
        [*scalars, order],
        (rows,),
        [e1, q, u, mixed, *rest],
        [row_spec] * 4 + [ANY] * len(rest),
        [narrow, narrow, states],
        [row_spec, row_spec, state_spec],
        [pltpu.VMEM((features, features), LOW), pltpu.SemaphoreType.DMA((len(rest),))],
        2 * count * features * (features + head_dim),
    )
    pins = []
    if by_hand:
        second_sent = channel_grads.forward(local_grad), down_sum.share(local_grad)
        sent_o, *kept_o = block_grads(
            after(gated_turned, *second_sent), [(e1, None)], order, "both"
        )
        received_o = moved(sent_o, "core")
        pins = [sent_o]
    state_grad, message = hop(local_grad, -1, *pins)
    dq, dk_part, dv_part = call(
        functools.partial(back_mixing_kernel, docs, tile, heads),
        scalars,
        (rows,),
        [q, q_slope, k, v, after(dmixed, message), state_in.astype(LOW)],
        [row_spec] * 5 + [state_spec],
        [narrow] * 3,
        [row_spec] * 3,
        [square] * 2,
        12 * count * features * tokens,
    )
    pins = [dq]
    if by_hand:
        channel_part = channel_grads.finish(dq)
        channel_sum = SeqSum(channel_part)
        down_total = down_sum.finish(dq)
        sent_uq, *kept_uq = block_grads(
            after(h_turned, channel_part), [(du, None), (dq, None)], order, "both"
        )
        received_uq = moved(sent_uq, "core")
        pins = [sent_uq]
    for _ in range(hops - 1):
        received, message = hop(message, -1)
        state_grad = state_grad + after(received, *pins)
    dk, dv = call(
        functools.partial(back_finish_kernel, docs, heads),
        scalars,
        (rows,),
        [k, k_slope, v, dk_part, dv_part, state_grad.astype(LOW)],
        [row_spec] * 5 + [state_spec],
        [narrow] * 2,
        [row_spec] * 2,
        [],
        4 * count * features * head_dim,
    )
    if by_hand:
        outer_grads = Scatter(
            [jnp.concatenate([a, b]) for a, b in zip(kept_uq, kept_o)],
            jnp.concatenate([received_uq, received_o]),
        )
        begun = outer_grads.begin(dk)
        sent_kv, *kept_kv = block_grads(
            after(h_turned, *begun), [(dk, None), (dv, None)], order, "both"
        )
        inner_grads = Scatter(kept_kv, moved(sent_kv, "core"))
        begun = outer_grads.forward(sent_kv), *inner_grads.begin(sent_kv)
        begun = *begun, channel_sum.share(sent_kv)
        dq = after(dq, *begun)
    upstream = mixer_back([dq, dk, dv, du], x, e1, key_value, rest, order, big)
    if by_hand:
        outer_part = outer_grads.finish(upstream)
        outer_sum = SeqSum(outer_part)
        begun = inner_grads.forward(upstream), outer_part
        y = down_forward(after(first, *begun), second, x1, down, order, big)
        inner_part = inner_grads.finish(y)
        inner_sum = SeqSum(inner_part)
        outer_total = outer_sum.share(inner_part)
        channel_total = channel_sum.finish(outer_total)
        inner_total = inner_sum.share(outer_total)
        outer_total = outer_sum.finish(inner_total)
        inner_total = inner_sum.finish(inner_total)
        mixer_gradient = jnp.stack(
            [outer_total[1], inner_total[0], inner_total[1], outer_total[0], outer_total[2]]
        )
    else:
        mixer_gradient = jnp.concatenate(
            [scattered_plainly(h_turned, [dq, dk, dv, du]), scattered_plainly(gated_turned, [e1])]
        )
        mixer_gradient = lax.psum(mixer_gradient, "seq")
    by_row = (rows, tokens, features)
    return (
        y.reshape(by_row),
        upstream.reshape(by_row),
        mixer_gradient.astype(WIDE)[None],
        channel_total.astype(WIDE).reshape(channel_in_weights.shape),
        down_total.astype(WIDE).reshape(channel_out_weights.shape),
    )


def solution(mesh):
    in_specs = (
        P("dp", "seq", None),
        P(None, None, "dp", None),
        P(None, None, "dp", None),
        P(None, "dp", None),
        P(),
        P("dp", None),
        P("dp", "seq", None),
    )
    out_specs = (
        P("dp", "seq", None),
        P("dp", "seq", None),
        P(None, None, "dp", None),
        P(None, None, "dp", None),
        P(None, "dp", None),
    )
    return jax.shard_map(local, mesh=mesh, in_specs=in_specs, out_specs=out_specs, check_vma=False)
```

```python
import functools
import math

import jax
import jax.numpy as jnp
from jax import lax
from jax.experimental import pallas as pl
from jax.experimental.pallas import tpu as pltpu
from jax.sharding import PartitionSpec as P

EPS = 1e-06
LONGEST_DOC = 1024
LOW = jnp.bfloat16
WIDE = jnp.float32
VMEM_BYTES = 60 * 1024 * 1024
WEIGH = 4
ANY = pl.BlockSpec(memory_space=pl.ANY)


def dot(left, right, left_dim=1, right_dim=0):
    return lax.dot_general(
        left, right, (((left_dim,), (right_dim,)), ((), ())), preferred_element_type=WIDE
    )


def shaped(*shape, kind=LOW):
    return jax.ShapeDtypeStruct(shape, kind)


def vmem_needed(arrays, specs, scratch, spare):
    total = spare
    for array, spec in zip(arrays, specs):
        if spec.block_shape is not None:
            total += 2 * math.prod(spec.block_shape) * array.dtype.itemsize
    for ref in scratch:
        if ref.memory_space == pltpu.VMEM:
            total += math.prod(ref.shape) * jnp.dtype(ref.dtype).itemsize
    return min(total, VMEM_BYTES)


def call(kernel, scalars, grid, inputs, in_specs, outputs, out_specs, scratch, flops, spare=8):
    size = sum(a.size * a.dtype.itemsize for a in (*inputs, *outputs))
    limit = vmem_needed((*inputs, *outputs), (*in_specs, *out_specs), scratch, spare << 20)
    return pl.pallas_call(
        kernel,
        out_shape=outputs,
        grid_spec=pltpu.PrefetchScalarGridSpec(
            num_scalar_prefetch=len(scalars),
            grid=grid,
            in_specs=in_specs,
            out_specs=out_specs,
            scratch_shapes=scratch,
        ),
        compiler_params=pltpu.CompilerParams(vmem_limit_bytes=limit),
        cost_estimate=pl.CostEstimate(
            flops=int(flops) * WEIGH, bytes_accessed=int(size) * WEIGH, transcendentals=0
        ),
    )(*scalars, *inputs)


def rows_spec(tile, width):
    return pl.BlockSpec((tile, width), lambda i, *_: (i, 0))


def after(value, *others):
    return lax.optimization_barrier((value, *others))[0]


def piece_copies(order_ref, pieces, layers, columns, into_ref, sems):
    parts = []
    for piece in pieces:
        stacked = len(piece.shape) == 4
        parts += [piece.at[i] for i in range(piece.shape[0])] if stacked else [piece]
    copies = []
    for index, part in enumerate(parts):
        rows = part.shape[1]
        at = pl.ds(pl.multiple_of(order_ref[index] * rows, rows), rows)
        copies.append(
            pltpu.make_async_copy(
                part.at[layers, :, columns], into_ref.at[..., at, :], sems.at[index]
            )
        )
    return copies


def piece_count(pieces):
    return sum(piece.shape[0] if piece.ndim == 4 else 1 for piece in pieces)


def started(copies):
    for copy in copies:
        copy.start()


def finished(copies):
    for copy in copies:
        copy.wait()


def doc_bounds(lengths_ref, row, docs, start, count):
    last = start + count - 1
    end = jnp.int32(0)
    last_from = jnp.int32(0)
    entry_to = jnp.int32(0)
    found = jnp.int32(0)
    for index in range(docs):
        end = end + lengths_ref[row, index]
        last_from = jnp.where(end <= last, end, last_from)
        ends_later = end > start - 1
        entry_to = jnp.where(ends_later & (found == 0), end, entry_to)
        found = jnp.where(ends_later, 1, found)
    return last_from - start, entry_to - start


def doc_starts(lengths_ref, row, docs, start, places):
    end = jnp.int32(0)
    begin = jnp.full(places.shape, -start, jnp.int32)
    for index in range(docs):
        end = end + lengths_ref[row, index]
        begin = jnp.where(places >= end - start, end - start, begin)
    return begin


def column(count, first=0):
    return first + lax.broadcasted_iota(jnp.int32, (count, 1), 0)


def project_kernel(tokens, tile, count, order_ref, h_ref, table_ref, *refs):
    pieces, (left_ref, slope_ref, right_ref, w_ref, sems) = refs[:count], refs[count:]
    step, width = pl.program_id(0), left_ref.shape[1]

    def copies(at):
        columns = pl.ds(pl.multiple_of(at * width, width), width)
        return piece_copies(
            order_ref, pieces, pl.ds(0, 2), columns, w_ref.at[at], sems.at[at]
        )

    @pl.when(step == 0)
    def _():
        for at in range(w_ref.shape[0]):
            started(copies(at))

    finished(copies(step))
    for first in range(0, h_ref.shape[0], tile):
        at = slice(first, first + tile)
        h = h_ref[at, :]
        pre = dot(h, w_ref[step, 0])
        gate = jax.nn.sigmoid(pre)
        decay = table_ref[first % tokens : first % tokens + tile, :].astype(WIDE)
        left_ref[at, :] = (pre * gate * decay).astype(LOW)
        slope_ref[at, :] = (gate * (1.0 + pre * (1.0 - gate)) * decay).astype(LOW)
        right_ref[at, :] = dot(h, w_ref[step, 1]).astype(LOW)


def project(h, table, pieces, order, tokens, tile):
    count, features = h.shape
    width = min(512, features)
    steps = features // width
    out = shaped(count, features)
    block = pl.BlockSpec((count, width), lambda i, *_: (0, i))
    return call(
        functools.partial(project_kernel, tokens, tile, len(pieces)),
        [order],
        (steps,),
        [h, table, *pieces],
        [
            pl.BlockSpec((count, features), lambda i, *_: (0, 0)),
            pl.BlockSpec((tokens, width), lambda i, *_: (0, i)),
            *[ANY] * len(pieces),
        ],
        [out] * 3,
        [block] * 3,
        [
            pltpu.VMEM((steps, 2, features, width), LOW),
            pltpu.SemaphoreType.DMA((steps, piece_count(pieces))),
        ],
        4 * count * features * features,
    )


def state_kernel(docs, start_ref, into_ref, out_ref, lengths_ref, k_ref, v_ref, state_ref):
    count, head_dim = k_ref.shape[0], state_ref.shape[-1]
    last_from, _ = doc_bounds(lengths_ref, pl.program_id(0), docs, start_ref[0], count)
    mask = jnp.broadcast_to((column(count) >= last_from).astype(WIDE), (count, head_dim))
    for head in range(state_ref.shape[1]):
        span = slice(head * head_dim, (head + 1) * head_dim)
        keys = (k_ref[:, span].astype(WIDE) * mask).astype(LOW)
        state_ref[0, head] = (dot(keys, v_ref[:, span], 0, 0) * out_ref[head]).astype(LOW)


def mixing_kernel(
    docs, tile, heads, start_ref, into_ref, out_ref, lengths_ref, q_ref, k_ref, v_ref, o_ref, mask_ref
):
    count, features = q_ref.shape
    head_dim = features // heads
    places = column(count)
    begin = doc_starts(lengths_ref, pl.program_id(0), docs, start_ref[0], places)
    across = lax.broadcasted_iota(jnp.int32, (count, count), 1)
    mask_ref[...] = ((across <= places) & (across >= begin)).astype(WIDE)
    for head in range(heads):
        span = slice(head * head_dim, (head + 1) * head_dim)
        for first in range(0, count, tile):
            upto = first + tile
            scores = dot(q_ref[first:upto, span], k_ref[:upto, span], 1, 1)
            scores = (scores * mask_ref[first:upto, :upto]).astype(LOW)
            o_ref[first:upto, span] = dot(scores, v_ref[:upto, span]).astype(LOW)


def norm_factor(value_rows):
    return lax.rsqrt(jnp.mean(value_rows * value_rows, axis=-1, keepdims=True) + EPS)


def norm_back(value_rows, upstream):
    factor = norm_factor(value_rows)
    inner = jnp.mean(upstream * value_rows, axis=-1, keepdims=True)
    return factor * upstream - (factor * factor * factor * inner) * value_rows


def finish_kernel(
    docs,
    tokens,
    heads,
    count,
    start_ref,
    into_ref,
    out_ref,
    lengths_ref,
    order_ref,
    q_ref,
    u_ref,
    part_ref,
    x_ref,
    state_ref,
    *refs,
):
    pieces = refs[:count]
    mixed_ref, gated_ref, x1_ref, h2_ref, h2_turned_ref, whole_ref, w_ref, sems = refs[count:]
    tile, features = q_ref.shape
    head_dim = features // heads
    step, steps = pl.program_id(0), tokens // tile
    layer = pieces[0].shape[-3] - 1
    copies = piece_copies(order_ref, pieces, layer, pl.ds(0, features), w_ref, sems)

    @pl.when(step == 0)
    def _():
        started(copies)

    row = step // steps
    _, entry_to = doc_bounds(lengths_ref, row, docs, start_ref[0], tokens)
    mask = (column(tile, (step % steps) * tile) < entry_to).astype(WIDE)
    mask = jnp.broadcast_to(mask, (tile, head_dim))
    for head in range(heads):
        span = slice(head * head_dim, (head + 1) * head_dim)
        state = (state_ref[0, head].astype(WIDE) * into_ref[head]).astype(LOW)
        whole_ref[:, span] = part_ref[:, span].astype(WIDE) + dot(q_ref[:, span], state) * mask
    mixed = whole_ref[...]
    mixed_ref[...] = mixed.astype(LOW)
    gated = (mixed * norm_factor(mixed) * u_ref[...].astype(WIDE)).astype(LOW)
    gated_ref[...] = gated.T

    @pl.when(step == 0)
    def _():
        finished(copies)

    x1 = x_ref[...].astype(WIDE) + dot(gated, w_ref[...])
    x1_ref[...] = x1.astype(LOW)
    h2 = (x1 * norm_factor(x1)).astype(LOW)
    h2_ref[...] = h2
    h2_turned_ref[...] = h2.T


def pair_kernel(tile, count, order_ref, h_ref, *refs):
    pieces, (first_ref, second_ref, turned_ref, w_ref, sems) = refs[:count], refs[count:]
    step, width = pl.program_id(0), first_ref.shape[1]

    def copies(at, layer):
        columns = pl.ds(pl.multiple_of(at * width, 128), width)
        return piece_copies(
            order_ref, pieces, layer, columns, w_ref.at[at, layer], sems.at[at, layer]
        )

    @pl.when(step == 0)
    def _():
        for at in range(w_ref.shape[0]):
            for layer in range(2):
                started(copies(at, layer))

    finished(copies(step, 0))
    first = dot(h_ref[...], w_ref[step, 0])
    first_ref[...] = first.astype(LOW)
    finished(copies(step, 1))
    for begin in range(0, h_ref.shape[0], tile):
        at = slice(begin, begin + tile)
        second = dot(h_ref[at, :], w_ref[step, 1])
        second_ref[at, :] = second.astype(LOW)
        turned_ref[:, at] = (first_ref[at, :].astype(WIDE) * second).astype(LOW).T


def pair(h, pieces, order, tile):
    (count, features), hidden = h.shape, pieces[0].shape[-1]
    steps = 2 if hidden % 256 == 0 else 1
    width, many = hidden // steps, len(pieces)
    block = pl.BlockSpec((count, width), lambda i, *_: (0, i))
    return call(
        functools.partial(pair_kernel, tile, many),
        [order],
        (steps,),
        [h, *pieces],
        [pl.BlockSpec((count, features), lambda i, *_: (0, 0)), *[ANY] * many],
        [shaped(count, hidden), shaped(count, hidden), shaped(hidden, count)],
        [block, block, pl.BlockSpec((width, count), lambda i, *_: (i, 0))],
        [
            pltpu.VMEM((steps, 2, features, width), LOW),
            pltpu.SemaphoreType.DMA((steps, 2, many)),
        ],
        4 * count * features * hidden,
    )


def down_back_kernel(count, order_ref, first_ref, second_ref, dy_ref, *refs):
    pieces, (dpair_ref, w_ref, sems) = refs[:count], refs[count:]
    copies = piece_copies(order_ref, pieces, 0, pl.ds(0, w_ref.shape[1]), w_ref, sems)

    @pl.when(pl.program_id(0) == 0)
    def _():
        started(copies)
        finished(copies)

    grad = dot(dy_ref[...], w_ref[...], 1, 1)
    dpair_ref[0] = (grad * second_ref[...].astype(WIDE)).astype(LOW)
    dpair_ref[1] = (grad * first_ref[...].astype(WIDE)).astype(LOW)


def down_back(first, second, dy, pieces, order, tile):
    (count, hidden), features = first.shape, dy.shape[1]
    wide, narrow = rows_spec(tile, hidden), rows_spec(tile, features)
    return call(
        functools.partial(down_back_kernel, len(pieces)),
        [order],
        (count // tile,),
        [first, second, dy, *pieces],
        [wide, wide, narrow, *[ANY] * len(pieces)],
        [shaped(2, count, hidden)],
        [pl.BlockSpec((2, tile, hidden), lambda i, *_: (0, i, 0))],
        [pltpu.VMEM((hidden, features), LOW), pltpu.SemaphoreType.DMA((len(pieces),))],
        2 * count * features * hidden,
    )[0]


def down_kernel(count, order_ref, first_ref, second_ref, x1_ref, *refs):
    pieces, (y_ref, w_ref, sems) = refs[:count], refs[count:]
    copies = piece_copies(order_ref, pieces, 0, pl.ds(0, w_ref.shape[1]), w_ref, sems)

    @pl.when(pl.program_id(0) == 0)
    def _():
        started(copies)
        finished(copies)

    glu = (first_ref[...].astype(WIDE) * second_ref[...].astype(WIDE)).astype(LOW)
    y_ref[...] = (x1_ref[...].astype(WIDE) + dot(glu, w_ref[...])).astype(LOW)


def down_forward(first, second, x1, pieces, order, tile):
    (count, hidden), features = first.shape, x1.shape[1]
    wide, narrow = rows_spec(tile, hidden), rows_spec(tile, features)
    return call(
        functools.partial(down_kernel, len(pieces)),
        [order],
        (count // tile,),
        [first, second, x1, *pieces],
        [wide, wide, narrow, *[ANY] * len(pieces)],
        [shaped(count, features)],
        [narrow],
        [pltpu.VMEM((hidden, features), LOW), pltpu.SemaphoreType.DMA((len(pieces),))],
        2 * count * features * hidden,
    )[0]


def pair_back_kernel(count, order_ref, dpair_ref, x1_ref, dy_ref, *refs):
    pieces, (e1_ref, w_ref, sems) = refs[:count], refs[count:]
    step = pl.program_id(0)

    def copies(layer):
        return piece_copies(
            order_ref, pieces, layer, pl.ds(0, w_ref.shape[2]), w_ref.at[layer], sems.at[layer]
        )

    @pl.when(step == 0)
    def _():
        started(copies(0))
        started(copies(1))
        finished(copies(0))

    total = dot(dpair_ref[0], w_ref[0], 1, 1)

    @pl.when(step == 0)
    def _():
        finished(copies(1))

    total = total + dot(dpair_ref[1], w_ref[1], 1, 1)
    e1 = dy_ref[...].astype(WIDE) + norm_back(x1_ref[...].astype(WIDE), total)
    e1_ref[...] = e1.astype(LOW)


def pair_back(dpair, x1, dy, pieces, order, tile):
    (_, count, hidden), features, many = dpair.shape, x1.shape[1], len(pieces)
    narrow = rows_spec(tile, features)
    return call(
        functools.partial(pair_back_kernel, many),
        [order],
        (count // tile,),
        [dpair, x1, dy, *pieces],
        [
            pl.BlockSpec((2, tile, hidden), lambda i, *_: (0, i, 0)),
            narrow,
            narrow,
            *[ANY] * many,
        ],
        [shaped(count, features)],
        [narrow],
        [pltpu.VMEM((2, features, hidden), LOW), pltpu.SemaphoreType.DMA((2, many))],
        4 * count * features * hidden,
    )[0]


def back_gate_kernel(
    docs,
    heads,
    count,
    start_ref,
    into_ref,
    out_ref,
    lengths_ref,
    order_ref,
    e1_ref,
    q_ref,
    u_ref,
    mixed_ref,
    *refs,
):
    pieces, (dmixed_ref, du_ref, grad_ref, w_ref, sems) = refs[:count], refs[count:]
    tokens, features = q_ref.shape
    head_dim = features // heads
    layer = pieces[0].shape[-3] - 1
    copies = piece_copies(order_ref, pieces, layer, pl.ds(0, features), w_ref, sems)

    @pl.when(pl.program_id(0) == 0)
    def _():
        started(copies)
        finished(copies)

    dgated = dot(e1_ref[...], w_ref[...], 1, 1)
    mixed = mixed_ref[...].astype(WIDE)
    du_ref[...] = (dgated * (mixed * norm_factor(mixed))).astype(LOW)
    dmixed_ref[...] = norm_back(mixed, dgated * u_ref[...].astype(WIDE)).astype(LOW)
    _, entry_to = doc_bounds(lengths_ref, pl.program_id(0), docs, start_ref[0], tokens)
    mask = jnp.broadcast_to((column(tokens) < entry_to).astype(WIDE), (tokens, head_dim))
    for head in range(heads):
        span = slice(head * head_dim, (head + 1) * head_dim)
        queries = (q_ref[:, span].astype(WIDE) * mask).astype(LOW)
        grad_ref[0, head] = (dot(queries, dmixed_ref[:, span], 0, 0) * into_ref[head]).astype(LOW)


def back_mixing_kernel(
    docs,
    tile,
    heads,
    start_ref,
    into_ref,
    out_ref,
    lengths_ref,
    q_ref,
    slope_ref,
    k_ref,
    v_ref,
    dmixed_ref,
    state_ref,
    dq_ref,
    dk_ref,
    dv_ref,
    mask_ref,
    turned_ref,
):
    count, features = q_ref.shape
    head_dim = features // heads
    row, start = pl.program_id(0), start_ref[0]
    _, entry_to = doc_bounds(lengths_ref, row, docs, start, count)
    places = column(count)
    begin = doc_starts(lengths_ref, row, docs, start, places)
    across = lax.broadcasted_iota(jnp.int32, (count, count), 1)
    mask_ref[...] = ((across <= places) & (across >= begin)).astype(WIDE)
    flat = lax.broadcasted_iota(jnp.int32, (1, count), 1)
    begin = doc_starts(lengths_ref, row, docs, start, flat)
    down = lax.broadcasted_iota(jnp.int32, (count, count), 0)
    turned_ref[...] = ((down <= flat) & (down >= begin)).astype(WIDE)
    entry = jnp.broadcast_to((places < entry_to).astype(WIDE), (count, head_dim))
    for head in range(heads):
        span = slice(head * head_dim, (head + 1) * head_dim)
        state = (state_ref[0, head].astype(WIDE) * into_ref[head]).astype(LOW)
        for first in range(0, count, tile):
            upto = first + tile
            here = slice(first, upto)
            grads = dot(dmixed_ref[here, span], v_ref[:upto, span], 1, 1)
            dq = dot((grads * mask_ref[here, :upto]).astype(LOW), k_ref[:upto, span])
            dq = dq + dot(dmixed_ref[here, span], state, 1, 1) * entry[here]
            dq_ref[here, span] = (dq * slope_ref[here, span].astype(WIDE)).astype(LOW)
            turned = turned_ref[here, first:]
            grads = dot(v_ref[here, span], dmixed_ref[first:, span], 1, 1) * turned
            dk_ref[here, span] = dot(grads.astype(LOW), q_ref[first:, span]).astype(LOW)
            scores = dot(k_ref[here, span], q_ref[first:, span], 1, 1) * turned
            dv_ref[here, span] = dot(scores.astype(LOW), dmixed_ref[first:, span]).astype(LOW)


def back_finish_kernel(
    docs,
    heads,
    start_ref,
    into_ref,
    out_ref,
    lengths_ref,
    k_ref,
    slope_ref,
    v_ref,
    dk_part_ref,
    dv_part_ref,
    grad_ref,
    dk_ref,
    dv_ref,
):
    count, features = k_ref.shape
    head_dim = features // heads
    last_from, _ = doc_bounds(lengths_ref, pl.program_id(0), docs, start_ref[0], count)
    mask = jnp.broadcast_to((column(count) >= last_from).astype(WIDE), (count, head_dim))
    for head in range(heads):
        span = slice(head * head_dim, (head + 1) * head_dim)
        grad = (grad_ref[0, head].astype(WIDE) * out_ref[head]).astype(LOW)
        dk = dot(v_ref[:, span], grad, 1, 1) * mask + dk_part_ref[:, span].astype(WIDE)
        dk_ref[:, span] = (dk * slope_ref[:, span].astype(WIDE)).astype(LOW)
        dv = dot(k_ref[:, span], grad) * mask + dv_part_ref[:, span].astype(WIDE)
        dv_ref[:, span] = dv.astype(LOW)


def mixer_back_kernel(count, last, order_ref, *refs):
    grads, refs = refs[:2], refs[2:]
    if last:
        (back_ref, x_ref, e1_ref), refs = refs[:3], refs[3:]
    pieces, (out_ref, w_ref, sems) = refs[:count], refs[count:]
    step, features = pl.program_id(0), out_ref.shape[1]

    def copies(index):
        return piece_copies(
            order_ref, pieces, index, pl.ds(0, features), w_ref.at[index], sems.at[index]
        )

    @pl.when(step == 0)
    def _():
        started(copies(0))
        started(copies(1))
        finished(copies(0))

    total = dot(grads[0][...], w_ref[0], 1, 1)

    @pl.when(step == 0)
    def _():
        finished(copies(1))

    total = total + dot(grads[1][...], w_ref[1], 1, 1)
    if last:
        total = total + back_ref[...]
        total = e1_ref[...].astype(WIDE) + norm_back(x_ref[...].astype(WIDE), total)
    out_ref[...] = total


def mixer_back(grads, pieces, order, tile, *others):
    count, features = grads[0].shape
    spec = rows_spec(tile, features)
    return call(
        functools.partial(mixer_back_kernel, len(pieces), bool(others)),
        [order],
        (count // tile,),
        [*grads, *others, *pieces],
        [spec] * (2 + len(others)) + [ANY] * len(pieces),
        [shaped(count, features, kind=WIDE)],
        [spec],
        [
            pltpu.VMEM((2, features, features), LOW),
            pltpu.SemaphoreType.DMA((2, piece_count(pieces))),
        ],
        4 * count * features * features,
    )[0]


def norm_kernel(x_ref, h_ref, turned_ref):
    x = x_ref[...].astype(WIDE)
    h = (x * norm_factor(x)).astype(LOW)
    h_ref[...] = h
    turned_ref[...] = h.T


def normed(x, tile):
    count, features = x.shape
    spec = rows_spec(tile, features)
    return call(
        norm_kernel,
        [],
        (count // tile,),
        [x],
        [spec],
        [shaped(count, features), shaped(features, count)],
        [spec, pl.BlockSpec((features, tile), lambda i, *_: (0, i))],
        [],
        0,
    )


def cast_kernel(layers_ref, in_ref, out_ref):
    out_ref[...] = in_ref[...].astype(LOW)


def cast(array, layers):
    block = (1, *array.shape[1:])
    return call(
        cast_kernel,
        [jnp.asarray(layers, jnp.int32)],
        (len(layers),),
        [array],
        [pl.BlockSpec(block, lambda i, layers: (layers[i], 0, 0))],
        [shaped(len(layers), *array.shape[1:])],
        [pl.BlockSpec(block, lambda i, *_: (i, 0, 0))],
        [],
        0,
    )[0]


def block_grads_kernel(layers, mode, order_ref, turned_ref, *refs):
    members = len(layers)
    rights, refs = refs[:members], refs[members:]
    if mode == "keep":
        add_ref, *refs = refs
    *out_refs, left_ref, right_ref, left_sems, sems = refs
    member, half, at = pl.program_id(0), pl.program_id(1), pl.program_id(2)
    halves, whole = left_ref.shape[:2]
    width, tile, steps = whole // 4, right_ref.shape[-1], right_ref.shape[1]

    def left_copy(part, index):
        block = order_ref[part * 4 + index] * width
        return pltpu.make_async_copy(
            turned_ref.at[pl.ds(pl.multiple_of(block, width), width), :],
            left_ref.at[part, pl.ds(index * width, width), :],
            left_sems.at[part, index],
        )

    def right_copy(index, step):
        right = rights[index] if layers[index] is None else rights[index].at[layers[index]]
        return pltpu.make_async_copy(
            right.at[:, pl.ds(pl.multiple_of(step * tile, 128), tile)],
            right_ref.at[index, step],
            sems.at[index, step],
        )

    @pl.when((member == 0) & (half == 0) & (at == 0))
    def _():
        for index in range(4):
            left_copy(0, index).start()
        for index in range(members):
            for step in range(steps):
                right_copy(index, step).start()
        if halves == 2:
            for index in range(4):
                left_copy(1, index).start()
        for index in range(4):
            left_copy(0, index).wait()

    if halves == 2:

        @pl.when((member == 0) & (half == 1) & (at == 0))
        def _():
            for index in range(4):
                left_copy(1, index).wait()

    for index in range(members):

        @pl.when((member == index) & (half == 0))
        def _(index=index):
            right_copy(index, at).wait()

    term = dot(left_ref[half], right_ref[member, at])
    if mode == "keep":
        term = term + add_ref[0].astype(WIDE)
    term = term.astype(LOW)

    def keep(refs):
        for index, ref in enumerate(refs):
            ref[0] = term[index * width : (index + 1) * width]

    if mode == "send":
        out_refs[0][0] = term
    elif mode == "keep":
        keep(out_refs)
    else:

        @pl.when(half == 0)
        def _():
            out_refs[0][0] = term

        @pl.when(half == 1)
        def _():
            keep(out_refs[1:])


def block_grads(turned, rights, order, mode, received=None):
    (features, count), columns = turned.shape, rights[0][0].shape[-1]
    width, members = features // 8, len(rights)
    halves = 2 if mode == "both" else 1
    order = {"send": order[4:], "keep": order[:4], "both": jnp.roll(order, -4)}[mode]
    steps = 2 if columns % 256 == 0 and (columns > 1024 or members == 1) else 1
    tile, whole = columns // steps, features // 2

    def sent(i, part, j, *_):
        return i, 0, jnp.where(part == 0, j, steps - 1)

    def kept(i, part, j, *_):
        return i, 0, jnp.where(part == halves - 1, j, 0)

    send = shaped(members, whole, columns), pl.BlockSpec((1, whole, tile), sent)
    keep = shaped(members, width, columns), pl.BlockSpec((1, width, tile), kept)
    results = {"send": [send], "keep": [keep] * 4, "both": [send] + [keep] * 4}[mode]
    extra = [received] if mode == "keep" else []
    return call(
        functools.partial(block_grads_kernel, [layer for _, layer in rights], mode),
        [order],
        (members, halves, steps),
        [turned, *(right for right, _ in rights), *extra],
        [ANY] * (1 + members) + [send[1]] * len(extra),
        [shape for shape, _ in results],
        [spec for _, spec in results],
        [
            pltpu.VMEM((halves, whole, count), LOW),
            pltpu.VMEM((members, steps, count, tile), LOW),
            pltpu.SemaphoreType.DMA((halves, 4)),
            pltpu.SemaphoreType.DMA((members, steps)),
        ],
        2 * members * halves * count * whole * columns,
    )


def passed_along(value, steps):
    count = lax.axis_size("seq")
    leading, last = max(0, -steps), min(count, count - steps)
    return lax.ppermute(value, "seq", [(source, source + steps) for source in range(leading, last)])


def hops_needed(tokens):
    return min((LONGEST_DOC - 2) // tokens + 1, lax.axis_size("seq") - 1)


def side_steps(device):
    return (2, 4) if device % 2 == 0 else (4, 2)


def moved(value, kind):
    count = lax.axis_size("dp")
    if kind == "core":
        pairs = [(device, device ^ 1) for device in range(count)]
    else:
        pairs = [(device, device ^ side_steps(device)[kind]) for device in range(count)]
    return lax.ppermute(value, "dp", pairs)


def block_order():
    device = lax.axis_index("dp")
    table = []
    for index in range(8):
        row = []
        for mine in (index, index ^ 1):
            first, second = side_steps(mine)
            row += [mine, mine ^ first, mine ^ second, mine ^ first ^ second]
        table.append(row)
    return jnp.asarray(table, jnp.int32)[device]


class SeqSum:
    def __init__(self, *values):
        self.totals, self.step = list(values), 0
        self.send()

    def send(self):
        pairs = [[(0, 1), (3, 2)], [(1, 2), (2, 1)], [(1, 0), (2, 3)]][self.step]
        self.received = [lax.ppermute(total, "seq", pairs) for total in self.totals]

    def on(self, *others):
        received = after(tuple(self.received), *others)
        self.totals = [plus(a, b) for a, b in zip(self.totals, received)]
        self.step += 1
        self.send()
        return tuple(self.totals)

    def finish(self, *others):
        place = lax.axis_index("seq")
        outside = (place == 0) | (place == 3)
        received = after(tuple(self.received), *others)
        return [
            jnp.where(outside, a, b).astype(WIDE) for a, b in zip(received, self.totals)
        ]


class SeqHalves:
    def __init__(self, value):
        self.odd = lax.axis_index("seq") % 2
        self.shape = value.shape
        halves = value.reshape(value.shape[0], 2, value.shape[1] // 2, value.shape[2])
        self.total = lax.dynamic_index_in_dim(halves, self.odd, 1, keepdims=False)
        self.received = self.swapped(lax.dynamic_index_in_dim(halves, 1 - self.odd, 1, False), 1)

    def swapped(self, value, step):
        return lax.ppermute(value, "seq", [(i, i ^ step) for i in range(4)])

    def on(self, step, *others):
        self.total = plus(self.total, after(self.received, *others))
        self.received = self.swapped(self.total, step)
        return self.total

    def finish(self, *others):
        received = after(self.received, *others)
        pair = [self.total.astype(WIDE), received.astype(WIDE)]
        halves = [lax.select_n(self.odd, *pair), lax.select_n(self.odd, *pair[::-1])]
        return jnp.stack(halves, axis=1).reshape(self.shape)


def plus(*terms):
    return sum(term.astype(WIDE) for term in terms).astype(LOW)


class Scatter:
    def __init__(self, kept, received=None):
        self.kept, self.received = kept, received

    def block(self, index):
        if self.received is None:
            return [self.kept[index]]
        width = self.kept[index].shape[1]
        return [self.kept[index], self.received[:, index * width : (index + 1) * width]]

    def begin(self, *others):
        received = self.received
        if received is not None:
            self.received = after(received, *others)
        message = jnp.stack([plus(*self.block(3)), plus(*self.block(1))])
        self.from_side = moved(message, 0)
        return message

    def forward(self, *others):
        self.from_side = after(self.from_side, *others)
        second = plus(*self.block(2), self.from_side[0])
        self.from_second = moved(second, 1)
        return second

    def finish(self, *others):
        return plus(*self.block(0), self.from_side[1], after(self.from_second, *others))


def scattered_plainly(left, rights):
    terms = [
        lax.dot_general(left, right, (((1,), (0,)), ((), ())), preferred_element_type=WIDE)
        for right in rights
    ]
    return lax.psum_scatter(jnp.stack(terms).astype(LOW), "dp", scatter_dimension=1, tiled=True)


def local(
    hidden_in,
    mixer_weights,
    channel_in_weights,
    channel_out_weights,
    decay_rates,
    doc_lengths,
    out_cotangent,
):
    rows, tokens, features = hidden_in.shape
    heads = decay_rates.shape[1]
    head_dim = features // heads
    docs = doc_lengths.shape[1]
    count = rows * tokens
    tile = min(256, tokens)
    by_hand = lax.axis_size("dp") == 8 and lax.axis_size("seq") == 4
    order = block_order() if by_hand else jnp.zeros((1,), jnp.int32)
    rates = decay_rates[0]
    start = lax.axis_index("seq") * jnp.asarray(tokens, jnp.int32)
    centre = tokens // 2
    into = jnp.exp(-rates * (centre + 1))
    out = jnp.exp(-rates * (tokens - 1 - centre))
    scalars = [start[None], into, out, doc_lengths]
    ends = jnp.cumsum(doc_lengths, axis=1, dtype=jnp.int32)
    doc_before = jnp.sum((ends <= start - 1).astype(jnp.int32), axis=1)
    doc_last = jnp.sum((ends <= start + tokens - 1).astype(jnp.int32), axis=1)
    passing = jnp.where(
        (doc_before == doc_last)[:, None], jnp.exp(-rates * tokens)[None, :], 0.0
    )
    centred = (jnp.arange(tokens, dtype=jnp.int32) - centre).astype(WIDE)[:, None]
    spread = jnp.repeat(rates, head_dim)[None, :] * centred
    query_table, key_table = jnp.exp(-spread), jnp.exp(spread)

    big = min(512, count)

    def hop(message, steps, *others):
        received = after(passed_along(message, steps), *others).astype(WIDE)
        return received, (passing[..., None, None] * received).astype(LOW)

    def gather(piece, *others):
        if not by_hand:
            return [lax.all_gather(piece, "dp", axis=1, tiled=True)]
        piece = after(piece, *others) if others else piece
        return [piece, moved(piece, 0), moved(piece, 1)]

    def forward(pieces, *others):
        if not by_hand:
            return pieces
        mine = [*pieces, moved(pieces[1], 1)]
        return mine + [moved(jnp.stack(after(tuple(mine), *others)), "core")]

    def gathered(piece):
        return [lax.all_gather(piece, "dp", axis=1, tiled=True)]

    first_order = jnp.zeros((1,), jnp.int32)
    mixer = mixer_weights[0]
    key_value = forward(gather(cast(mixer, (1, 2))))
    channel = gathered(channel_in_weights[0].astype(LOW))
    down = gathered(channel_out_weights.astype(LOW))
    rest = gather(cast(mixer, (0, 3, 4)), *key_value[1:4])

    x = hidden_in.reshape(count, features)
    h, h_turned = normed(x, tile)
    dy = out_cotangent.reshape(count, features)
    narrow, turned_out = shaped(count, features), shaped(features, count)
    states = shaped(rows, heads, head_dim, head_dim)
    row_spec = rows_spec(tokens, features)
    state_spec = pl.BlockSpec((1, heads, head_dim, head_dim), lambda i, *_: (i, 0, 0, 0))
    square = pltpu.VMEM((tokens, tokens), WIDE)
    hops = hops_needed(tokens)

    k, k_slope, v = project(h, key_table, key_value, order, tokens, tile)
    if by_hand:
        rest[1] = after(rest[1], k)
    local_state = call(
        functools.partial(state_kernel, docs),
        scalars,
        (rows,),
        [after(k, *rest[1:2]) if by_hand else k, v],
        [row_spec] * 2,
        [states],
        [state_spec],
        [],
        2 * count * features * head_dim,
    )[0]
    rest = forward(rest, local_state)
    state_in, message = hop(local_state, 1)
    q, q_slope, u = project(after(h, message), query_table, rest, order, tokens, tile)
    part = call(
        functools.partial(mixing_kernel, docs, tile, heads),
        scalars,
        (rows,),
        [q, k, v],
        [row_spec] * 3,
        [narrow],
        [row_spec],
        [square],
        4 * count * features * tokens,
    )[0]
    for _ in range(hops - 1):
        received, message = hop(message, 1)
        state_in = state_in + after(received, part)
    spec = rows_spec(tile, features)
    turned_spec = pl.BlockSpec((features, tile), lambda i, *_: (0, i))
    steps = tokens // tile
    mixed, gated_turned, x1, h2, h2_turned = call(
        functools.partial(finish_kernel, docs, tokens, heads, len(rest)),
        [*scalars, order],
        (count // tile,),
        [q, u, part, x, state_in.astype(LOW), *rest],
        [spec] * 4
        + [
            pl.BlockSpec(
                (1, heads, head_dim, head_dim), lambda i, *_: (i // steps, 0, 0, 0)
            )
        ]
        + [ANY] * len(rest),
        [narrow, turned_out, narrow, narrow, turned_out],
        [spec, turned_spec, spec, spec, turned_spec],
        [
            pltpu.VMEM((tile, features), WIDE),
            pltpu.VMEM((features, features), LOW),
            pltpu.SemaphoreType.DMA((piece_count(rest),)),
        ],
        2 * count * features * (features + head_dim),
    )
    first, second, turned = pair(h2, channel, first_order, tile)

    down_grads = channel_grads = outer_grads = inner_grads = None
    if by_hand:
        sent, *kept = block_grads(turned, [(dy, None)], order, "both")
        down_grads = Scatter(kept, moved(sent, "core"))
        first = after(first, sent)
    dpair = down_back(first, second, dy, down, first_order, big)
    if by_hand:
        rights = [(dpair, 0), (dpair, 1)]
        begun = down_grads.begin(dpair)
        [sent] = block_grads(after(h2_turned, begun), rights, order, "send")
        received = moved(sent, "core")
        e1 = pair_back(after(dpair, sent), x1, dy, channel, first_order, big)
        begun = down_grads.forward(e1)
        channel_grads = Scatter(
            block_grads(after(h2_turned, begun), rights, order, "keep", received)
        )
        begun = channel_grads.begin()
        down_part = down_grads.finish(*channel_grads.kept)
        down_sum = SeqSum(down_part)
        e1 = after(e1, down_part, begun)
    else:
        y = down_forward(first, second, x1, down, first_order, big)
        down_total = lax.psum(scattered_plainly(turned, [dy]), "seq")
        e1 = pair_back(dpair, x1, dy, channel, first_order, big)
        channel_total = lax.psum(scattered_plainly(h2_turned, [dpair[0], dpair[1]]), "seq")
    dmixed, du, local_grad = call(
        functools.partial(back_gate_kernel, docs, heads, len(rest)),
        [*scalars, order],
        (rows,),
        [e1, q, u, mixed, *rest],
        [row_spec] * 4 + [ANY] * len(rest),
        [narrow, narrow, states],
        [row_spec, row_spec, state_spec],
        [pltpu.VMEM((features, features), LOW), pltpu.SemaphoreType.DMA((piece_count(rest),))],
        2 * count * features * (features + head_dim),
    )
    pins = []
    if by_hand:
        second_sent = down_sum.on(local_grad)
        sent_o, *kept_o = block_grads(
            after(gated_turned, *second_sent), [(e1, None)], order, "both"
        )
        received_o = moved(sent_o, "core")
        pins = [sent_o]
    state_grad, message = hop(local_grad, -1, *pins)
    dq, dk_part, dv_part = call(
        functools.partial(back_mixing_kernel, docs, tile, heads),
        scalars,
        (rows,),
        [q, q_slope, k, v, after(dmixed, message), state_in.astype(LOW)],
        [row_spec] * 5 + [state_spec],
        [narrow] * 3,
        [row_spec] * 3,
        [square] * 2,
        12 * count * features * tokens,
    )
    pins = [dq]
    if by_hand:
        channel_part = channel_grads.forward(dq), *down_sum.on(dq)
        sent_uq, *kept_uq = block_grads(
            after(h_turned, *channel_part), [(du, None), (dq, None)], order, "both"
        )
        received_uq = moved(sent_uq, "core")
        pins = [sent_uq]
    for _ in range(hops - 1):
        received, message = hop(message, -1)
        state_grad = state_grad + after(received, *pins)
    dk, dv = call(
        functools.partial(back_finish_kernel, docs, heads),
        scalars,
        (rows,),
        [k, k_slope, v, dk_part, dv_part, state_grad.astype(LOW)],
        [row_spec] * 5 + [state_spec],
        [narrow] * 2,
        [row_spec] * 2,
        [],
        4 * count * features * head_dim,
    )
    if by_hand:
        outer_grads = Scatter(
            [jnp.concatenate([a, b]) for a, b in zip(kept_uq, kept_o)],
            jnp.concatenate([received_uq, received_o]),
        )
        channel_part = channel_grads.finish(dk)
        channel_sum = SeqSum(channel_part[:1], channel_part[1:])
        begun = outer_grads.begin(dk), channel_part
        sent_kv, *kept_kv = block_grads(
            after(h_turned, *begun), [(dk, None), (dv, None)], order, "both"
        )
        inner_grads = Scatter(kept_kv, moved(sent_kv, "core"))
        du = after(du, sent_kv)
    back = mixer_back([dq, du], rest, order, big)
    if by_hand:
        begun = inner_grads.begin(back), outer_grads.forward(back), *channel_sum.on(back)
        dk = after(dk, *begun)
    upstream = mixer_back([dk, dv], key_value, order, big, back, x, e1)
    if by_hand:
        outer_part = outer_grads.finish(upstream)
        outer_sum = SeqHalves(outer_part)
        begun = inner_grads.forward(upstream), outer_part, *channel_sum.on(upstream)
        y = down_forward(after(first, *begun), second, x1, down, first_order, big)
        inner_part = inner_grads.finish(y)
        inner_sum = SeqHalves(inner_part)
        down_total = down_sum.finish(y)[0]
        outer_sum.on(2, inner_part)
        inner_sum.on(2, inner_part)
        outer_sum.on(1)
        inner_sum.on(1)
        channel_total = jnp.concatenate(channel_sum.finish(y))
        outer_total, inner_total = outer_sum.finish(), inner_sum.finish()
        mixer_gradient = jnp.stack(
            [outer_total[1], inner_total[0], inner_total[1], outer_total[0], outer_total[2]]
        )
    else:
        mixer_gradient = jnp.concatenate(
            [scattered_plainly(h_turned, [dq, dk, dv, du]), scattered_plainly(gated_turned, [e1])]
        )
        mixer_gradient = lax.psum(mixer_gradient, "seq")
    by_row = (rows, tokens, features)
    return (
        y.reshape(by_row),
        upstream.reshape(by_row),
        mixer_gradient.astype(WIDE)[None],
        channel_total.astype(WIDE).reshape(channel_in_weights.shape),
        down_total.astype(WIDE).reshape(channel_out_weights.shape),
    )


def solution(mesh):
    in_specs = (
        P("dp", "seq", None),
        P(None, None, "dp", None),
        P(None, None, "dp", None),
        P(None, "dp", None),
        P(),
        P("dp", None),
        P("dp", "seq", None),
    )
    out_specs = (
        P("dp", "seq", None),
        P("dp", "seq", None),
        P(None, None, "dp", None),
        P(None, None, "dp", None),
        P(None, "dp", None),
    )
    return jax.shard_map(local, mesh=mesh, in_specs=in_specs, out_specs=out_specs, check_vma=False)
```
